32 devices in a mesh: grp: 2 (over y), seq: 4 (over z), head: 2 (over x), dat: 2 (over core).
Axes of the slice: x: 2, y: 2, z: 4, core: 2. Of those that a mesh axis runs over, the one named last changes fastest.
Arguments:
- queries: bfloat16 [4, 256, 3072], P(('grp', 'dat'), 'seq', 'head'), parts along dimension 0, may hold values from -10 to 10
- keys: bfloat16 [4, 256, 512], P(('grp', 'dat'), 'seq', 'head'), parts along dimension 0, may hold values from -6 to 6
- values: bfloat16 [4, 256, 512], P(('grp', 'dat'), 'seq', 'head'), parts along dimension 0, may hold values from -6 to 6
- residual_in: bfloat16 [4, 256, 3072], P(('grp', 'dat'), 'seq', 'head'), parts along dimension 0, may hold values from -40 to 40
- out_proj: bfloat16 [24, 128, 3072], P('head', 'seq'), may hold values from -0.5 to 0.5
- norm_gain: bfloat16 [3072], replicated, may hold values from 0.5 to 1.5
- expert_gate: bfloat16 [4, 3072, 8192], P('head', None, 'seq'), may hold values from -0.109375 to 0.109375
- expert_up: bfloat16 [4, 3072, 8192], P('head', None, 'seq'), may hold values from -0.109375 to 0.109375
- routes: int32 [4, 256, 2], P(('grp', 'dat'), 'seq'), parts along dimension 0, may hold values from 0 to 3, as said below
- gate_numer: int32 [4, 256], P(('grp', 'dat'), 'seq'), parts along dimension 0, may hold values from 64 to 191
- sequence_lengths: int32 [4], P(('grp', 'dat')), parts along dimension 0, may hold values from 128 to 256, as said below
Outputs:
- stream: bfloat16 [4, 256, 3072], P(('grp', 'dat'), 'seq', 'head'), parts along dimension 0
- expert_hidden: bfloat16 [4, 4, 160, 8192], P('head', ('grp', 'dat'), None, 'seq'), parts along dimension 1
The draws below stay inside these ranges and needn't reach their ends.
There are 2 independent parts, one for each index of `grp`. The reference program is written for one: setup_inputs(seed, part) draws one part's arguments, and reference() takes and returns one part's arrays. A program takes and returns all parts, laid end to end along the dimension named above; an argument that names none is the same for every part. Nothing has to cross between parts.
Inputs may be any that keep to these rules, and one draw needn't show every extreme that they name: `routes`: for each sequence one expert is named by exactly 40 tokens of every aligned block of 64 positions, every other expert by at most 40 tokens of such a block; the two experts of a token differ. `sequence_lengths`: one sequence of the batch has the full length 256.
All inputs are finite; a program needn't handle non-finite values.
Results may differ from the reference program's by a relative error of at most 0.019.
Values may be sent and summed in bfloat16 or wider, within the bound.
A program may use at most 128 MiB of HBM per device.

```python
import math
import jax
import jax.numpy as jnp
from jax import lax

D = 3072
QUERY_HEAD_COUNT = 24
KEY_VALUE_HEADS = 4
HEAD_SIZE = 128
EXPERTS = 4
FF = 8192
TOK_DEV = 64
MOST = 40
SEQUENCE_LENGTH = 256
SLOTS = 160
BATCH_SEQUENCES = 2
N_SEQ = 4


def draw_queries(key, part):
    array_shape = (BATCH_SEQUENCES, SEQUENCE_LENGTH, QUERY_HEAD_COUNT * HEAD_SIZE)
    draws = jnp.clip(jax.random.normal(jax.random.fold_in(key, 11), array_shape, jnp.float32), -6.0, 6.0)
    return draws.astype(jnp.bfloat16)


def draw_keys(key, part):
    array_shape = (BATCH_SEQUENCES, SEQUENCE_LENGTH, KEY_VALUE_HEADS * HEAD_SIZE)
    draws = jnp.clip(jax.random.normal(jax.random.fold_in(key, 21), array_shape, jnp.float32), -6.0, 6.0)
    return draws.astype(jnp.bfloat16)


def draw_residual_in(key, part):
    array_shape = (BATCH_SEQUENCES, SEQUENCE_LENGTH, D)
    col_frac = jnp.arange(D, dtype=jnp.float32) / D
    row_scale = jnp.exp(jax.random.uniform(jax.random.fold_in(key, 31), (BATCH_SEQUENCES, SEQUENCE_LENGTH, 1), jnp.float32, math.log(0.3), math.log(3.0)))
    col_scale = 10.0 ** (col_frac - 0.7)
    noise_part = jnp.clip(jax.random.normal(jax.random.fold_in(key, 34), array_shape, jnp.float32), -6.0, 6.0)
    values = noise_part * col_scale * row_scale
    return values.astype(jnp.bfloat16)


def block_ranks(sub_key):
    return jax.random.permutation(sub_key, TOK_DEV)


def draw_routes(key, part):
    per_row = SEQUENCE_LENGTH // TOK_DEV
    blocks = BATCH_SEQUENCES * per_row
    others = EXPERTS - 1
    hot_expert = jnp.repeat(jax.random.randint(jax.random.fold_in(key, 41), (BATCH_SEQUENCES, 1), 0, EXPERTS), per_row, axis=0)
    rank_in_block = jax.vmap(block_ranks)(jax.random.split(jax.random.fold_in(key, 42), blocks)).astype(jnp.int32)
    turn_first = jax.random.randint(jax.random.fold_in(key, 43), (blocks, 1), 0, others)
    turn_second = jax.random.randint(jax.random.fold_in(key, 44), (blocks, 1), 0, others)
    in_hot = rank_in_block < MOST
    rest = rank_in_block - MOST
    partner = (hot_expert + 1 + (rank_in_block + turn_first) % others) % EXPERTS
    first_other = (hot_expert + 1 + (rest + turn_second) % others) % EXPERTS
    second_other = (hot_expert + 1 + (rest + turn_second + 1) % others) % EXPERTS
    first_pick = jnp.where(in_hot, hot_expert, first_other)
    second = jnp.where(in_hot, partner, second_other)
    flip_order = jax.random.randint(jax.random.fold_in(key, 45), (blocks, TOK_DEV), 0, 2) == 1
    lead = jnp.where(flip_order, second, first_pick)
    trail = jnp.where(flip_order, first_pick, second)
    return jnp.stack([lead, trail], axis=-1).reshape(BATCH_SEQUENCES, SEQUENCE_LENGTH, 2).astype(jnp.int32)


def draw_sequence_lengths(key, part):
    lengths_drawn = jax.random.randint(jax.random.fold_in(key, 51), (BATCH_SEQUENCES,), SEQUENCE_LENGTH // 2, SEQUENCE_LENGTH + 1)
    full_row = jax.random.randint(jax.random.fold_in(key, 52), (), 0, BATCH_SEQUENCES)
    return jnp.where(jnp.arange(BATCH_SEQUENCES) == full_row, SEQUENCE_LENGTH, lengths_drawn).astype(jnp.int32)


def plant(values, stream_key, least, high):
    shape = values.shape
    index_at = [jax.random.randint(jax.random.fold_in(stream_key, axis), (), 0, shape[axis]) for axis in range(len(shape))]
    values = values.at[tuple(index_at)].set(least)
    longest = shape.index(max(shape))
    index_at[longest] = (index_at[longest] + 1) % shape[longest]
    return values.at[tuple(index_at)].set(high)


def level_of(own_key, extent, cuts, least, largest):
    loudness, own = 1.0, jax.random.fold_in(own_key, 6)
    for dim, blocks in cuts:
        heights = jnp.exp(jax.random.uniform(jax.random.fold_in(own, dim), (blocks,), jnp.float32, least / len(cuts), largest / len(cuts)))
        loudness = loudness * jnp.repeat(heights, extent[dim] // blocks).reshape([-1 if axis == dim else 1 for axis in range(len(extent))])
    return loudness


def gaussian(key, extent, spread, most, pieces=(), kind=jnp.bfloat16):
    values = spread * jax.random.normal(key, extent, jnp.float32)
    if pieces:
        values = values * level_of(key, extent, pieces, -0.22, 0.18)
    return jnp.clip(values, -most, most).astype(kind)


def setup_inputs(seed: int = 0, part: int = 0) -> dict:
    splits = jax.random.split(jax.random.key(seed), 12)
    own_keys = jax.random.split(jax.random.fold_in(splits[11], part), 12)
    queries = draw_queries(jax.random.fold_in(jax.random.fold_in(splits[11], part), 71), part)
    keys = draw_keys(jax.random.fold_in(jax.random.fold_in(splits[11], part), 71), part)
    values = gaussian(own_keys[2], (BATCH_SEQUENCES, SEQUENCE_LENGTH, KEY_VALUE_HEADS * HEAD_SIZE), 1.0, 6.0, ((0, 2), (1, 4), (2, 2)))
    residual_in = draw_residual_in(jax.random.fold_in(jax.random.fold_in(splits[11], part), 71), part)
    out_proj = gaussian(splits[4], (QUERY_HEAD_COUNT, HEAD_SIZE, D), HEAD_SIZE ** -0.5, 0.5, ((0, 2), (1, 4)))
    norm_gain = jnp.clip(1.0 + 0.1 * jax.random.normal(splits[5], (D,), jnp.float32), 0.5, 1.5).astype(jnp.bfloat16)
    expert_gate = gaussian(splits[6], (EXPERTS, D, FF), D ** -0.5, 0.109375, ((0, 2), (2, 4)))
    expert_up = gaussian(splits[7], (EXPERTS, D, FF), D ** -0.5, 0.109375, ((0, 2), (2, 4)))
    routes = draw_routes(jax.random.fold_in(jax.random.fold_in(splits[11], part), 71), part)
    gate_numer = plant(jax.random.randint(own_keys[9], (BATCH_SEQUENCES, SEQUENCE_LENGTH), 64, 192), jax.random.fold_in(own_keys[9], 1), 64, 191).astype(jnp.int32)
    sequence_lengths = draw_sequence_lengths(jax.random.fold_in(jax.random.fold_in(splits[11], part), 71), part)
    return dict(queries=queries, keys=keys, values=values, residual_in=residual_in, out_proj=out_proj, norm_gain=norm_gain, expert_gate=expert_gate, expert_up=expert_up, routes=routes, gate_numer=gate_numer, sequence_lengths=sequence_lengths)


EPS = 1e-05
NEG = -1e+30

def slot_sources(marked, capacity):
    tok_len = marked.shape[1]
    counted = jnp.cumsum(marked, axis=1)
    rank_ids = jnp.arange(capacity, dtype=jnp.int32)
    source = lax.optimization_barrier(jnp.sum((counted[:, None, :] <= rank_ids[None, :, None]).astype(jnp.int32), axis=2))
    filled = rank_ids[None, :] < counted[:, -1:]
    source = jnp.minimum(source, tok_len - 1).astype(jnp.int32)
    return (source, filled)

def expert_rows(rows_in, slot_gate, gate_matrix, up_matrix):
    gate_part = jnp.dot(rows_in, gate_matrix, preferred_element_type=jnp.float32)
    up_part = jnp.dot(rows_in, up_matrix, preferred_element_type=jnp.float32)
    return (slot_gate[:, None] * (jax.nn.silu(gate_part) * up_part)).astype(jnp.bfloat16)

def reference(queries, keys, values, residual_in, out_proj, norm_gain, expert_gate, expert_up, routes, gate_numer, sequence_lengths):
    heads_per_group = QUERY_HEAD_COUNT // KEY_VALUE_HEADS
    score_scale = 1.0 / math.sqrt(HEAD_SIZE)
    positions = jnp.arange(SEQUENCE_LENGTH, dtype=jnp.int32)
    grouped_queries = queries.reshape(BATCH_SEQUENCES, SEQUENCE_LENGTH, KEY_VALUE_HEADS, heads_per_group, HEAD_SIZE).transpose(0, 2, 1, 3, 4).reshape(BATCH_SEQUENCES * KEY_VALUE_HEADS, SEQUENCE_LENGTH, heads_per_group, HEAD_SIZE)
    grouped_keys = keys.reshape(BATCH_SEQUENCES, SEQUENCE_LENGTH, KEY_VALUE_HEADS, HEAD_SIZE).transpose(0, 2, 1, 3).reshape(BATCH_SEQUENCES * KEY_VALUE_HEADS, SEQUENCE_LENGTH, HEAD_SIZE)
    grouped_values = values.reshape(BATCH_SEQUENCES, SEQUENCE_LENGTH, KEY_VALUE_HEADS, HEAD_SIZE).transpose(0, 2, 1, 3).reshape(BATCH_SEQUENCES * KEY_VALUE_HEADS, SEQUENCE_LENGTH, HEAD_SIZE)
    group_bounds = jnp.repeat(sequence_lengths, KEY_VALUE_HEADS)

    def attend(inputs):
        query_block, key_block, value_block, valid_len = inputs
        scores = jnp.einsum('thd,nd->htn', query_block.astype(jnp.float32), key_block.astype(jnp.float32), precision=lax.Precision.HIGHEST) * score_scale
        allowed = (positions[None, :] <= positions[:, None]) & (positions < valid_len)[None, :]
        scores = jnp.where(allowed[None], scores, NEG)
        top_score = lax.optimization_barrier(jnp.max(scores, axis=-1, keepdims=True))
        weights = jnp.where(allowed[None], jnp.exp(scores - top_score), 0.0)
        denom_sum = lax.optimization_barrier(jnp.sum(weights, axis=-1))
        rounded = lax.optimization_barrier(weights.astype(jnp.bfloat16)).astype(jnp.float32)
        weighted = jnp.einsum('htn,nd->thd', rounded, value_block.astype(jnp.float32), precision=lax.Precision.HIGHEST)
        return (weighted / denom_sum.T[:, :, None]).astype(jnp.bfloat16)
    attended_values = lax.map(attend, (grouped_queries, grouped_keys, grouped_values, group_bounds))
    attended_values = attended_values.reshape(BATCH_SEQUENCES, KEY_VALUE_HEADS, SEQUENCE_LENGTH, heads_per_group, HEAD_SIZE).transpose(0, 2, 1, 3, 4).reshape(BATCH_SEQUENCES * SEQUENCE_LENGTH, QUERY_HEAD_COUNT * HEAD_SIZE)
    mixed_sum = jnp.dot(attended_values, out_proj.reshape(QUERY_HEAD_COUNT * HEAD_SIZE, D), preferred_element_type=jnp.float32)
    stream = (residual_in.reshape(BATCH_SEQUENCES * SEQUENCE_LENGTH, D).astype(jnp.float32) + mixed_sum).astype(jnp.bfloat16)
    as_float = stream.astype(jnp.float32)
    mean_sq = lax.optimization_barrier(jnp.mean(as_float * as_float, axis=1, keepdims=True))
    normed = (as_float * lax.rsqrt(mean_sq + EPS) * norm_gain.astype(jnp.float32)).astype(jnp.bfloat16)
    first_weight = gate_numer.astype(jnp.float32) / 256.0
    blocks = BATCH_SEQUENCES * N_SEQ

    def one_expert(inputs):
        gate_matrix, up_matrix, expert_id = inputs
        gates = jnp.where(routes[..., 0] == expert_id, first_weight, 0.0) + jnp.where(routes[..., 1] == expert_id, 1.0 - first_weight, 0.0)
        marked = (gates > 0).astype(jnp.int32).reshape(blocks, TOK_DEV)
        source, filled = slot_sources(marked, MOST)
        flat_index = (jnp.arange(blocks, dtype=jnp.int32)[:, None] * TOK_DEV + source).reshape(-1)
        rows_in = jnp.take(normed, flat_index, axis=0)
        slot_gate = jnp.where(filled.reshape(-1), jnp.take(gates.reshape(-1), flat_index), 0.0)
        return expert_rows(rows_in, slot_gate, gate_matrix, up_matrix).reshape(BATCH_SEQUENCES, SLOTS, FF)
    hidden = lax.map(one_expert, (expert_gate, expert_up, jnp.arange(EXPERTS, dtype=jnp.int32)))
    return (stream.reshape(BATCH_SEQUENCES, SEQUENCE_LENGTH, D), hidden)
```

```python
import functools
import math

import jax
import jax.numpy as jnp
from jax import lax
from jax.experimental import pallas as pl
from jax.experimental.pallas import tpu as pltpu
from jax.sharding import PartitionSpec as P

HEAD_SIZE = 128
MOST = 40
EPS = 1e-05
NEG = -1e30
RING_BYTES = 40 * 1024 * 1024
UNITS = 24
MESH = pl.DeviceIdType.MESH
F32 = jnp.float32
BF16 = jnp.bfloat16


def unit_order(n, parts):
    units = [(b, c) for b in range(max(n - 2, 0)) for c in range(parts)]
    early = parts // 2
    units += [(n - 2, c) for c in range(early)] + [(n - 1, c) for c in range(early)]
    for c in range(early, parts):
        units += [(n - 2, c), (n - 1, c)]
    return units


def mix_kernel(
    n, m, nd, ng, pieces,
    len_ref, q_hbm, k_hbm, v_hbm, route_hbm, numer_hbm, res_hbm, gain_hbm, w_ref, wg_ref, wu_ref,
    own_ref, out_ref,
    q_ref, route_ref, numer_ref, res_ref, gain_ref,
    st, metas, meta_ref, tiles, acc, rows, sq, picks, gates,
    kvbuf, wbuf, cut, abuf, pbuf, sbuf, up, cross, hid,
    in_s, kv_s, kv_r, kf_s, me_s, me_r, w_s, w_r, wy_s, wy_r, wd_s, wd_r, wl,
    a_s, a_r, af_s, af_r, s_s, s_r, c_r, t_s, t_r, x_s, x_r, tile_s, out_s,
):
    z = lax.axis_index("seq")
    x = lax.axis_index("head")
    c_me = lax.axis_index("dat")
    g_me = lax.axis_index("grp")
    tok, share = res_ref.shape
    heads = q_ref.shape[1] // HEAD_SIZE
    kv = kvbuf.shape[2] // 2
    groups = kv // HEAD_SIZE
    per = heads // groups
    width = HEAD_SIZE // n
    parts, cw = st.shape[1], st.shape[4]
    depth = abuf.shape[3]
    experts, hidden = acc.shape[0], acc.shape[3]
    ring = tiles.shape[0]
    half = n // 2
    batch = 4 if n % 4 == 0 else n
    span, part_slots = batch * tok, batch * MOST

    lower = z < half
    inner = jnp.where(lower, z + 1, z - 1)
    outer = jnp.where(lower, z - 1, z + 1)
    middle = (z == half - 1) | (z == half)
    has_outer = (z > 0) & (z < n - 1)

    def peer(me, k, size):
        return lax.rem(me + k, size)

    def source(me, k, size):
        return lax.rem(me - k + size, size)

    sends = []

    def remote(src, dst, s_sem, r_sem, where):
        return pltpu.make_async_remote_copy(
            src_ref=src, dst_ref=dst, send_sem=s_sem, recv_sem=r_sem,
            device_id=where, device_id_type=MESH,
        )

    def send(src, dst, s_sem, r_sem, where, cond=None):
        make = functools.partial(remote, src, dst, s_sem, r_sem, where)
        if cond is None:
            make().start()
        else:
            pl.when(cond)(lambda: make().start())
        sends.append((cond, make))

    def arrived(dst, r_sem, where):
        remote(dst, dst, in_s.at[0], r_sem, where).wait_recv()

    order = [(c, e, u) for c in range(parts) for e in range(experts) for u in range(2)]

    def tile_copies(q):
        c, e, u = order[q]
        return [
            pltpu.make_async_copy(
                (wg_ref, wu_ref)[u].at[e, pl.ds(h * share + c * cw, cw), :],
                tiles.at[q % ring, pl.ds(h * cw, cw), :],
                tile_s.at[q % ring, h],
            )
            for h in range(m)
        ]

    barrier = pltpu.get_barrier_semaphore()
    count = 0
    for axis, me, size in (("seq", z, n), ("head", x, m), ("dat", c_me, nd), ("grp", g_me, ng)):
        for k in range(1, size):
            pl.semaphore_signal(barrier, inc=1, device_id={axis: peer(me, k, size)}, device_id_type=MESH)
            count += 1
    loads = [
        pltpu.make_async_copy(src, dst, in_s.at[i])
        for i, (src, dst) in enumerate((
            (k_hbm, kvbuf.at[z, :, pl.ds(0, kv)]), (v_hbm, kvbuf.at[z, :, pl.ds(kv, kv)]), (q_hbm, q_ref),
            (route_hbm, route_ref), (numer_hbm, numer_ref), (res_hbm, res_ref), (gain_hbm, gain_ref),
        ))
    ]
    for load in loads:
        load.start()
    own_w = []
    for c in range(parts):
        start = pl.multiple_of(x * share + c * cw, 128)
        own_w.append(pltpu.make_async_copy(w_ref.at[:, pl.ds(start, cw)], wbuf.at[x, c], wl.at[c]))
        own_w[-1].start()
    for s in range(n):
        @pl.when(s > z)
        def _(s=s):
            kvbuf[s] = jnp.zeros(kvbuf.shape[1:], BF16)
    for load in loads:
        load.wait()
    meta_ref[0:2] = route_ref[...].astype(F32)
    meta_ref[2:3] = numer_ref[...].astype(F32)
    meta_ref[3:8] = jnp.zeros((5, tok), F32)
    metas[z] = meta_ref[...]
    pl.semaphore_wait(barrier, count)

    for k in range(1, n):
        to = z + k
        at = jnp.minimum(to, n - 1)
        send(kvbuf.at[z], kvbuf.at[z], kv_s.at[k - 1], kv_r.at[z], {"seq": at}, (to < n) & ((z >= half) | (to <= half)))
    w_rows = depth // pieces
    piece = g_me * nd + c_me if pieces > 1 else 0

    def w_block(h, c, p):
        return wbuf.at[h, c, pl.ds(pl.multiple_of(p * w_rows, w_rows), w_rows), :]

    for c in range(parts):
        for j in range(1, m):
            to = peer(x, j, m)
            start = pl.multiple_of(to * share + c * cw, 128)
            src = w_ref.at[pl.ds(pl.multiple_of(piece * w_rows, w_rows), w_rows), pl.ds(start, cw)]
            send(src, w_block(x, c, piece), w_s.at[j - 1, c], w_r.at[j - 1, c], {"head": to})
    for k in range(1, n):
        send(meta_ref, metas.at[z], me_s.at[k - 1], me_r.at[z], {"seq": peer(z, k, n)})
    for q in range(min(ring, len(order))):
        for copy in tile_copies(q):
            copy.start()

    def w_over_x(c):
        for j in range(1, m):
            s = source(x, j, m)
            block = w_block(s, c, piece)
            arrived(block, w_r.at[j - 1, c], {"head": s})
            if pieces > 1:
                for k in range(1, ng):
                    send(block, block, wy_s.at[j - 1, c, k - 1], wy_r.at[j - 1, c, k - 1], {"grp": peer(g_me, k, ng)})
                for i in range(1, nd):
                    send(block, block, wd_s.at[j - 1, c, i - 1, 0], wd_r.at[j - 1, c, i - 1, 0], {"dat": peer(c_me, i, nd)})

    def w_over_y(c):
        if pieces == 1:
            return
        for j in range(1, m):
            s = source(x, j, m)
            for k in range(1, ng):
                g = source(g_me, k, ng)
                block = w_block(s, c, g * nd + c_me)
                arrived(block, wy_r.at[j - 1, c, k - 1], {"grp": g})
                for i in range(1, nd):
                    send(block, block, wd_s.at[j - 1, c, i - 1, k], wd_r.at[j - 1, c, i - 1, k], {"dat": peer(c_me, i, nd)})

    def w_ready(c):
        own_w[c].wait()
        if pieces == 1:
            return
        for j in range(1, m):
            s = source(x, j, m)
            for i in range(1, nd):
                d = source(c_me, i, nd)
                for k in range(ng):
                    g = source(g_me, k, ng)
                    arrived(w_block(s, c, g * nd + d), wd_r.at[j - 1, c, i - 1, k], {"dat": d})

    def attend():
        row = lax.broadcasted_iota(jnp.int32, (per * tok, n * tok), 0)
        col = lax.broadcasted_iota(jnp.int32, (per * tok, n * tok), 1)
        allowed = (col <= lax.rem(row, tok) + z * tok) & (col < len_ref[0])
        scale = 1.0 / math.sqrt(HEAD_SIZE)
        done = []
        for g in range(groups):
            lanes = slice(g * HEAD_SIZE, (g + 1) * HEAD_SIZE)
            queries = jnp.concatenate(
                [q_ref[:, (g * per + i) * HEAD_SIZE : (g * per + i + 1) * HEAD_SIZE] for i in range(per)], axis=0
            )
            keys = kvbuf[:, :, lanes].reshape(n * tok, HEAD_SIZE)
            vals = kvbuf[:, :, kv + g * HEAD_SIZE : kv + (g + 1) * HEAD_SIZE].reshape(n * tok, HEAD_SIZE)
            scores = lax.dot_general(queries, keys, (((1,), (1,)), ((), ())), preferred_element_type=F32) * scale
            scores = jnp.where(allowed, scores, NEG)
            top = jnp.max(scores, axis=1, keepdims=True)
            probs = jnp.where(allowed, jnp.exp(scores - top), 0.0)
            denom = jnp.sum(probs, axis=1, keepdims=True)
            mixed = jnp.dot(probs.astype(BF16), vals, preferred_element_type=F32)
            done.append((mixed / denom).astype(BF16))
        for d in range(n):
            cut[d] = jnp.concatenate(
                [
                    done[g][i * tok : (i + 1) * tok, d * width : (d + 1) * width]
                    for g in range(groups)
                    for i in range(per)
                ],
                axis=1,
            )
        abuf[x, z] = cut[z]

    def attention_sends():
        out = []
        for k in range(1, n):
            to = peer(z, k, n)
            out.append((cut.at[to], abuf.at[x, z], a_s.at[k - 1], a_r.at[z], {"seq": to}))
        for j in range(1, m):
            out.append((cut.at[z], abuf.at[x, z], af_s.at[j - 1, z], af_r.at[j - 1, z], {"head": peer(x, j, m)}))
        return out

    def attention_at(cond):
        @pl.when(cond)
        def _():
            for s in range(n):
                @pl.when(s < z)
                def _(s=s):
                    arrived(kvbuf.at[s], kv_r.at[s], {"seq": s})

                if s < half:
                    @pl.when(z == half)
                    def _(s=s):
                        for d in range(half + 1, n):
                            remote(kvbuf.at[s], kvbuf.at[s], kf_s.at[s, d - half - 1], kv_r.at[s], {"seq": d}).start()
            attend()
            for item in attention_sends():
                remote(*item).start()

    def forward(b):
        @pl.when(z != b)
        def _():
            arrived(abuf.at[x, b], a_r.at[b], {"seq": b})
            for j in range(1, m):
                remote(
                    abuf.at[x, b], abuf.at[x, b], af_s.at[j - 1, b], af_r.at[j - 1, b], {"head": peer(x, j, m)}
                ).start()

    def a_ready(b):
        for j in range(1, m):
            h = source(x, j, m)
            arrived(abuf.at[h, b], af_r.at[j - 1, b], {"head": h})

    def project(b, c):
        cols = slice(c * cw, (c + 1) * cw)
        total = res_ref[:, cols].astype(F32) * (z == b).astype(F32)
        for h in range(m):
            total = total + jnp.dot(abuf[h, b], wbuf[h, c], preferred_element_type=F32)
        pbuf[b, c] = total

    def to_inner(b, c):
        pl.when(middle)(lambda: remote(sbuf.at[b, c], cross.at[b, c], s_s.at[b, c], c_r.at[b, c], {"seq": inner}).start())
        if n > 2:
            pl.when(jnp.logical_not(middle))(
                lambda: remote(sbuf.at[b, c], up.at[b, c], s_s.at[b, c], s_r.at[b, c], {"seq": inner}).start()
            )

    def first(b, c):
        sbuf[b, c] = pbuf[b, c].astype(BF16)
        to_inner(b, c)

    def inwards(b, c):
        arrived(up.at[b, c], s_r.at[b, c], {"seq": outer})
        sbuf[b, c] = (pbuf[b, c] + up[b, c].astype(F32)).astype(BF16)
        to_inner(b, c)

    def outwards(b, c):
        mine = st.at[x, c, b]

        @pl.when(middle)
        def _():
            arrived(cross.at[b, c], c_r.at[b, c], {"seq": inner})
            st[x, c, b] = (sbuf[b, c].astype(F32) + cross[b, c].astype(F32)).astype(BF16)

        if n > 2:
            @pl.when(jnp.logical_not(middle))
            def _():
                arrived(mine, t_r.at[b, c], {"seq": inner})

            @pl.when(has_outer)
            def _():
                remote(mine, mine, t_s.at[b, c], t_r.at[b, c], {"seq": outer}).start()
        for j in range(1, m):
            remote(mine, mine, x_s.at[j - 1, b, c], x_r.at[j - 1, b, c], {"head": peer(x, j, m)}).start()

    def routing():
        for s in range(n):
            @pl.when(s != z)
            def _(s=s):
                arrived(metas.at[s], me_r.at[s], {"seq": s})
        r_id = lax.broadcasted_iota(jnp.int32, (span, span), 0)
        c_id = lax.broadcasted_iota(jnp.int32, (span, span), 1)
        before = ((r_id < c_id) & (r_id // tok == c_id // tok)).astype(BF16)
        slot_id = lax.broadcasted_iota(jnp.int32, (part_slots, span), 0)
        base = (lax.broadcasted_iota(jnp.int32, (1, span), 1) // tok) * MOST
        for b in range(n // batch):
            meta = jnp.concatenate([metas[b * batch + i] for i in range(batch)], axis=1)
            weight = meta[2:3] / 256.0
            for e in range(experts):
                this = (x * experts + e).astype(F32)
                gate = jnp.where(meta[0:1] == this, weight, 0.0) + jnp.where(meta[1:2] == this, 1.0 - weight, 0.0)
                marked = gate > 0
                spread = jnp.broadcast_to(jnp.where(marked, 1.0, 0.0), (8, span)).astype(BF16)
                rank = jnp.dot(spread, before, preferred_element_type=F32)[0:1].astype(jnp.int32)
                pick = jnp.where(slot_id == jnp.where(marked, rank + base, -1), 1.0, 0.0)
                picks[b, e * part_slots : (e + 1) * part_slots] = pick.astype(BF16)
                gates[e, b * part_slots : (b + 1) * part_slots] = jnp.sum(pick * gate, axis=1, keepdims=True)

    def gather(c):
        for b in range(n):
            for j in range(1, m):
                h = source(x, j, m)
                arrived(st.at[h, c, b], x_r.at[j - 1, b, c], {"head": h})
        for h in range(m):
            start = h * share + c * cw
            gain = gain_ref[start : start + cw].astype(F32).reshape(1, cw)
            for b in range(n // batch):
                block = st[h, c, b * batch : (b + 1) * batch].reshape(span, cw)
                raw = jnp.dot(picks[b], block, preferred_element_type=F32)
                square = raw * raw
                folded = square[:, 0:128]
                for i in range(1, cw // 128):
                    folded = folded + square[:, i * 128 : (i + 1) * 128]
                scaled = (raw * gain).astype(BF16)
                own = slice(b * part_slots, (b + 1) * part_slots)
                for e in range(experts):
                    mine = slice(e * part_slots, (e + 1) * part_slots)
                    rows[e, own, h * cw : (h + 1) * cw] = scaled[mine]
                    if c == 0 and h == 0:
                        sq[e, own] = folded[mine]
                    else:
                        sq[e, own] += folded[mine]

    def tile_of(c, e, u):
        return (c * experts + e) * 2 + u

    def multiply(c, e, u):
        q = tile_of(c, e, u)
        for copy in tile_copies(q):
            copy.wait()
        term = jnp.dot(rows[e], tiles[q % ring], preferred_element_type=F32)
        acc[e, u] = term if c == 0 else acc[e, u] + term
        if q + ring < len(order):
            for copy in tile_copies(q + ring):
                copy.start()

    def finish(c, e):
        for u in range(2):
            for copy in tile_copies(tile_of(c, e, u)):
                copy.wait()
        factor = lax.rsqrt(jnp.sum(sq[e], axis=1, keepdims=True) / (m * share) + EPS)
        step = min(hidden, 512)
        for t in range(hidden // step):
            cols = slice(t * step, (t + 1) * step)
            part = []
            for u in range(2):
                term = jnp.dot(rows[e], tiles[tile_of(c, e, u) % ring, :, cols], preferred_element_type=F32)
                part.append((term if c == 0 else acc[e, u, :, cols] + term) * factor)
            act = part[0] / (1.0 + jnp.exp(-part[0]))
            hid[e, :, cols] = (gates[e] * (act * part[1])).astype(BF16)
        copy = pltpu.make_async_copy(hid.at[e], out_ref.at[e, 0], out_s.at[e])
        copy.start()
        return copy

    units = unit_order(n, parts)
    total_units = len(units)
    late = max(n - 2, 0) * parts
    at_end = jnp.logical_not(has_outer)

    def of_block(b):
        return [(b, c) for c in range(parts)]

    def run(cond, events):
        if events:
            @pl.when(cond)
            def _():
                for f, u in events:
                    f(*u)

    def stage(b):
        a_ready(b)
        for c in range(parts):
            if b == 0:
                w_over_y(c)
                w_ready(c)
            project(b, c)
            if b < n - 2:
                run(at_end, [(first, (b, c))])
        if b == n - 2:
            run(at_end, [(first, (b, c)) for c in range(parts // 2)])
        if b == n - 1:
            run(at_end, [(first, u) for u in units[late + parts // 2 :]])

    attention_at(z == 0)
    for c in range(parts):
        w_over_x(c)
        if c == min(1, parts - 1):
            forward(0)
            for_zero = [s for s in range(1, n) if max(0, s - 2) == 0]
            attention_at((z >= 1) & (z <= for_zero[-1]))
    for b in range(n):
        if b > 0:
            forward(b)
            if b + 2 < n:
                attention_at(z == b + 2)
        if b == min(1, n - 1):
            routing()
        events = []
        if 2 <= b:
            a_list = of_block(b - 2)
            b_list = of_block(b - 3) if b >= 3 else []
            for i in range(parts):
                if b_list:
                    events.append((outwards, b_list[i]))
                events.append((inwards, a_list[i]))
        run(has_outer, events)
        stage(b)

    run(at_end, [(outwards, u) for u in units[:late]])
    events = []
    for i in range(parts):
        if n >= 3:
            events.append((outwards, of_block(n - 3)[i]))
            events.append((inwards, units[late + i]))
    run(has_outer, events)
    ready = [max(i for i, u in enumerate(units) if u[1] == c) for c in range(parts)]
    work = []
    for c in range(parts - 1):
        work.append((ready[c] + 5, functools.partial(gather, c)))
        for e in range(experts):
            work.append((ready[c] + 5, functools.partial(multiply, c, e, 0)))
            work.append((ready[c] + 5, functools.partial(multiply, c, e, 1)))
    for j in range(late, total_units):
        if j + parts < total_units and n >= 3:
            run(has_outer, [(inwards, units[j + parts])])
        outwards(*units[j])
        for _ in range(3):
            if work and work[0][0] <= j:
                work.pop(0)[1]()
    for _, f in work:
        f()
    gather(parts - 1)
    outs = []
    for c in range(parts):
        outs.append(pltpu.make_async_copy(st.at[x, c, z], own_ref.at[:, pl.ds(c * cw, cw)], out_s.at[experts + c]))
        outs[-1].start()
    for e in range(experts):
        outs.append(finish(parts - 1, e))

    for cond, make in sends:
        if cond is None:
            make().wait_send()
        else:
            pl.when(cond)(lambda make=make: make().wait_send())

    @pl.when(z == half)
    def _():
        for s in range(half):
            for d in range(half + 1, n):
                remote(kvbuf.at[s], kvbuf.at[s], kf_s.at[s, d - half - 1], kv_r.at[s], {"seq": d}).wait_send()

    for item in attention_sends():
        remote(*item).wait_send()
    for b in range(n):
        @pl.when(z != b)
        def _(b=b):
            for j in range(1, m):
                remote(
                    abuf.at[x, b], abuf.at[x, b], af_s.at[j - 1, b], af_r.at[j - 1, b], {"head": peer(x, j, m)}
                ).wait_send()
    for b, c in units:
        remote(sbuf.at[b, c], cross.at[b, c], s_s.at[b, c], c_r.at[b, c], {"seq": inner}).wait_send()
        mine = st.at[x, c, b]
        if n > 2:
            @pl.when(has_outer)
            def _(b=b, c=c, mine=mine):
                remote(mine, mine, t_s.at[b, c], t_r.at[b, c], {"seq": outer}).wait_send()
        for j in range(1, m):
            remote(mine, mine, x_s.at[j - 1, b, c], x_r.at[j - 1, b, c], {"head": peer(x, j, m)}).wait_send()
    for copy in outs:
        copy.wait()


def place_kernel(own_ref, hidden_ref, own_out, hidden_out, sems):
    first = pltpu.make_async_copy(own_ref, own_out, sems.at[0])
    second = pltpu.make_async_copy(hidden_ref, hidden_out, sems.at[1])
    first.start()
    second.start()
    first.wait()
    second.wait()


def local(
    n, m, nd, ng,
    queries, keys, values, residual_in, out_proj, norm_gain,
    expert_gate, expert_up, routes, gate_numer, sequence_lengths,
):
    tok, feats = queries.shape[1:]
    kv = keys.shape[2]
    share = residual_in.shape[2]
    heads, width, features = out_proj.shape
    depth = heads * width
    experts, _, hidden = expert_gate.shape
    slots = n * MOST
    batch = 4 if n % 4 == 0 else n
    parts = max(p for p in range(1, share // 128 + 1) if share % (128 * p) == 0 and (p == 1 or n * p <= UNITS))
    cw = share // parts
    pieces = ng * nd if depth % (16 * ng * nd) == 0 else 1
    ring = min(2 * parts * experts, RING_BYTES // (2 * m * cw * hidden))
    vmem = pl.BlockSpec(memory_space=pltpu.VMEM)
    hbm = pl.BlockSpec(memory_space=pl.ANY)
    dma = pltpu.SemaphoreType.DMA
    own, hidden_out = pl.pallas_call(
        functools.partial(mix_kernel, n, m, nd, ng, pieces),
        out_shape=(
            jax.ShapeDtypeStruct((tok, share), BF16),
            jax.ShapeDtypeStruct((experts, 1, slots, hidden), BF16),
        ),
        in_specs=[pl.BlockSpec(memory_space=pltpu.SMEM)] + [hbm] * 10,
        out_specs=(hbm, hbm),
        scratch_shapes=[
            pltpu.VMEM((tok, feats), BF16),
            pltpu.VMEM((2, tok), jnp.int32),
            pltpu.VMEM((1, tok), jnp.int32),
            pltpu.VMEM((tok, share), BF16),
            pltpu.VMEM((features,), BF16),
            pltpu.VMEM((m, parts, n, tok, cw), BF16),
            pltpu.VMEM((n, 8, tok), F32),
            pltpu.VMEM((8, tok), F32),
            pltpu.VMEM((ring, m * cw, hidden), BF16),
            pltpu.VMEM((experts, 2, slots, hidden), F32),
            pltpu.VMEM((experts, slots, m * cw), BF16),
            pltpu.VMEM((experts, slots, 128), F32),
            pltpu.VMEM((n // batch, experts * batch * MOST, batch * tok), BF16),
            pltpu.VMEM((experts, slots, 1), F32),
            pltpu.VMEM((n, tok, 2 * kv), BF16),
            pltpu.VMEM((m, parts, depth, cw), BF16),
            pltpu.VMEM((n, tok, depth), BF16),
            pltpu.VMEM((m, n, tok, depth), BF16),
            pltpu.VMEM((n, parts, tok, cw), F32),
            pltpu.VMEM((n, parts, tok, cw), BF16),
            pltpu.VMEM((n, parts, tok, cw), BF16),
            pltpu.VMEM((n, parts, tok, cw), BF16),
            pltpu.VMEM((experts, slots, hidden), BF16),
            dma((7,)),
            dma((n - 1,)), dma((n,)), dma((max(n // 2, 1), max(n - n // 2 - 1, 1))),
            dma((n - 1,)), dma((n,)),
            dma((m - 1, parts)), dma((m - 1, parts)),
            dma((m - 1, parts, max(ng - 1, 1))), dma((m - 1, parts, max(ng - 1, 1))),
            dma((m - 1, parts, max(nd - 1, 1), ng)), dma((m - 1, parts, max(nd - 1, 1), ng)),
            dma((parts,)),
            dma((n - 1,)), dma((n,)), dma((m - 1, n)), dma((m - 1, n)),
            dma((n, parts)), dma((n, parts)), dma((n, parts)),
            dma((n, parts)), dma((n, parts)),
            dma((m - 1, n, parts)), dma((m - 1, n, parts)),
            dma((ring, m)), dma((experts + parts,)),
        ],
        compiler_params=pltpu.CompilerParams(
            collective_id=0, has_side_effects=True, vmem_limit_bytes=63 * 1024 * 1024
        ),
    )(
        sequence_lengths, queries[0], keys[0], values[0], routes[0].T, gate_numer, residual_in[0],
        norm_gain, out_proj.reshape(depth, features), expert_gate, expert_up,
    )
    own, hidden_out = pl.pallas_call(
        place_kernel,
        out_shape=tuple(jax.ShapeDtypeStruct(a.shape, a.dtype) for a in (own, hidden_out)),
        in_specs=[vmem, vmem],
        out_specs=(hbm, hbm),
        scratch_shapes=[dma((2,))],
    )(own, hidden_out)
    return (own[None], hidden_out)


def solution(mesh):
    seq_spec = P(("grp", "dat"), "seq", "head")
    in_specs = (
        seq_spec, seq_spec, seq_spec, seq_spec,
        P("head", "seq", None), P(),
        P("head", None, "seq"), P("head", None, "seq"),
        P(("grp", "dat"), "seq", None), P(("grp", "dat"), "seq"), P(("grp", "dat")),
    )
    out_specs = (seq_spec, P("head", ("grp", "dat"), None, "seq"))
    sizes = [mesh.shape[axis] for axis in ("seq", "head", "dat", "grp")]
    body = functools.partial(local, *sizes)
    return jax.shard_map(body, mesh=mesh, in_specs=in_specs, out_specs=out_specs, check_vma=False)
```

```python
import functools
import math

import jax
import jax.numpy as jnp
from jax import lax
from jax.experimental import pallas as pl
from jax.experimental.pallas import tpu as pltpu
from jax.sharding import PartitionSpec as P

HEAD_SIZE = 128
MOST = 40
EPS = 1e-05
NEG = -1e30
RING_BYTES = 40 * 1024 * 1024
UNITS = 12
MESH = pl.DeviceIdType.MESH
F32 = jnp.float32
BF16 = jnp.bfloat16


def early_of(parts):
    return parts // 3


def unit_order(n, parts):
    units = [(b, c) for b in range(max(n - 2, 0)) for c in range(parts)]
    early = early_of(parts)
    units += [(n - 2, c) for c in range(early)] + [(n - 1, c) for c in range(early)]
    for c in range(early, parts):
        units += [(n - 2, c), (n - 1, c)]
    return units


def mix_kernel(
    n, m, nd, ng, pieces,
    len_ref, q_hbm, k_hbm, v_hbm, route_hbm, numer_hbm, res_hbm, gain_hbm, w_ref, wg_ref, wu_ref,
    own_ref, out_ref,
    q_ref, route_ref, numer_ref, res_ref, gain_ref,
    st, metas, meta_ref, tiles, acc, rows, sq, picks, gates,
    kvbuf, wbuf, cut, abuf, pbuf, sbuf, up, cross, hid,
    in_s, kv_s, kv_r, me_s, me_r, w_s, w_r, wy_s, wy_r, wd_s, wd_r, wl,
    a_s, a_r, af_s, af_r, s_s, s_r, c_r, t_s, t_r, x_s, x_r, tile_s, out_s,
):
    z = lax.axis_index("seq")
    x = lax.axis_index("head")
    c_me = lax.axis_index("dat")
    g_me = lax.axis_index("grp")
    tok, share = res_ref.shape
    heads = q_ref.shape[1] // HEAD_SIZE
    kv = kvbuf.shape[2] // 2
    groups = kv // HEAD_SIZE
    per = heads // groups
    width = HEAD_SIZE // n
    parts, cw = st.shape[1], st.shape[4]
    depth = abuf.shape[3]
    experts, hidden = acc.shape[0], acc.shape[3]
    ring = tiles.shape[0]
    half = n // 2
    batch = 4 if n % 4 == 0 else n
    span, part_slots = batch * tok, batch * MOST

    lower = z < half
    inner = jnp.where(lower, z + 1, z - 1)
    outer = jnp.where(lower, z - 1, z + 1)
    middle = (z == half - 1) | (z == half)
    has_outer = (z > 0) & (z < n - 1)

    def peer(me, k, size):
        return lax.rem(me + k, size)

    def source(me, k, size):
        return lax.rem(me - k + size, size)

    sends = []

    def remote(src, dst, s_sem, r_sem, where):
        return pltpu.make_async_remote_copy(
            src_ref=src, dst_ref=dst, send_sem=s_sem, recv_sem=r_sem,
            device_id=where, device_id_type=MESH,
        )

    def send(src, dst, s_sem, r_sem, where, cond=None):
        make = functools.partial(remote, src, dst, s_sem, r_sem, where)
        if cond is None:
            make().start()
        else:
            pl.when(cond)(lambda: make().start())
        sends.append((cond, make))

    def arrived(dst, r_sem, where):
        remote(dst, dst, in_s.at[0], r_sem, where).wait_recv()

    order = [(c, e, u) for c in range(parts) for e in range(experts) for u in range(2)]

    def tile_copies(q):
        c, e, u = order[q]
        return [
            pltpu.make_async_copy(
                (wg_ref, wu_ref)[u].at[e, pl.ds(h * share + c * cw, cw), :],
                tiles.at[q % ring, pl.ds(h * cw, cw), :],
                tile_s.at[q % ring, h],
            )
            for h in range(m)
        ]

    barrier = pltpu.get_barrier_semaphore()
    count = 0
    for axis, me, size in (("seq", z, n), ("head", x, m), ("dat", c_me, nd), ("grp", g_me, ng)):
        for k in range(1, size):
            pl.semaphore_signal(barrier, inc=1, device_id={axis: peer(me, k, size)}, device_id_type=MESH)
            count += 1
    loads = [
        pltpu.make_async_copy(src, dst, in_s.at[i])
        for i, (src, dst) in enumerate((
            (k_hbm, kvbuf.at[z, :, pl.ds(0, kv)]), (v_hbm, kvbuf.at[z, :, pl.ds(kv, kv)]), (q_hbm, q_ref),
            (route_hbm, route_ref), (numer_hbm, numer_ref), (res_hbm, res_ref), (gain_hbm, gain_ref),
        ))
    ]
    for load in loads:
        load.start()
    own_w = []
    for c in range(parts):
        start = pl.multiple_of(x * share + c * cw, 128)
        own_w.append(pltpu.make_async_copy(w_ref.at[:, pl.ds(start, cw)], wbuf.at[x, c], wl.at[c]))
        own_w[-1].start()
    for q in range(min(ring, len(order))):
        for copy in tile_copies(q):
            copy.start(priority=1)
    for s in range(n):
        @pl.when(s > z)
        def _(s=s):
            kvbuf[s] = jnp.zeros(kvbuf.shape[1:], BF16)
    for load in loads:
        load.wait()
    meta_ref[0:2] = route_ref[...].astype(F32)
    meta_ref[2:3] = numer_ref[...].astype(F32)
    meta_ref[3:8] = jnp.zeros((5, tok), F32)
    metas[z] = meta_ref[...]
    pl.semaphore_wait(barrier, count)

    for k in range(n - 1, 0, -1):
        to = jnp.minimum(z + k, n - 1)
        send(kvbuf.at[z], kvbuf.at[z], kv_s.at[k - 1], kv_r.at[z], {"seq": to}, z + k < n)
    w_rows = depth // pieces
    piece = g_me * nd + c_me if pieces > 1 else 0

    def w_block(h, c, p):
        return wbuf.at[h, c, pl.ds(pl.multiple_of(p * w_rows, w_rows), w_rows), :]

    for c in range(parts):
        for j in range(1, m):
            to = peer(x, j, m)
            start = pl.multiple_of(to * share + c * cw, 128)
            src = w_ref.at[pl.ds(pl.multiple_of(piece * w_rows, w_rows), w_rows), pl.ds(start, cw)]
            send(src, w_block(x, c, piece), w_s.at[j - 1, c], w_r.at[j - 1, c], {"head": to})
    for k in range(1, n):
        send(meta_ref, metas.at[z], me_s.at[k - 1], me_r.at[z], {"seq": peer(z, k, n)})

    def w_over_x(c):
        for j in range(1, m):
            s = source(x, j, m)
            block = w_block(s, c, piece)
            arrived(block, w_r.at[j - 1, c], {"head": s})
            if pieces > 1:
                for k in range(1, ng):
                    send(block, block, wy_s.at[j - 1, c, k - 1], wy_r.at[j - 1, c, k - 1], {"grp": peer(g_me, k, ng)})
                for i in range(1, nd):
                    send(block, block, wd_s.at[j - 1, c, i - 1, 0], wd_r.at[j - 1, c, i - 1, 0], {"dat": peer(c_me, i, nd)})

    def w_over_y(c):
        if pieces == 1:
            return
        for j in range(1, m):
            s = source(x, j, m)
            for k in range(1, ng):
                g = source(g_me, k, ng)
                block = w_block(s, c, g * nd + c_me)
                arrived(block, wy_r.at[j - 1, c, k - 1], {"grp": g})
                for i in range(1, nd):
                    send(block, block, wd_s.at[j - 1, c, i - 1, k], wd_r.at[j - 1, c, i - 1, k], {"dat": peer(c_me, i, nd)})

    def w_ready(c):
        own_w[c].wait()
        if pieces == 1:
            return
        for j in range(1, m):
            s = source(x, j, m)
            for i in range(1, nd):
                d = source(c_me, i, nd)
                for k in range(ng):
                    g = source(g_me, k, ng)
                    arrived(w_block(s, c, g * nd + d), wd_r.at[j - 1, c, i - 1, k], {"dat": d})

    def attend():
        row = lax.broadcasted_iota(jnp.int32, (per * tok, n * tok), 0)
        col = lax.broadcasted_iota(jnp.int32, (per * tok, n * tok), 1)
        allowed = (col <= lax.rem(row, tok) + z * tok) & (col < len_ref[0])
        scale = 1.0 / math.sqrt(HEAD_SIZE)
        done = []
        for g in range(groups):
            lanes = slice(g * HEAD_SIZE, (g + 1) * HEAD_SIZE)
            queries = jnp.concatenate(
                [q_ref[:, (g * per + i) * HEAD_SIZE : (g * per + i + 1) * HEAD_SIZE] for i in range(per)], axis=0
            )
            keys = kvbuf[:, :, lanes].reshape(n * tok, HEAD_SIZE)
            vals = kvbuf[:, :, kv + g * HEAD_SIZE : kv + (g + 1) * HEAD_SIZE].reshape(n * tok, HEAD_SIZE)
            scores = lax.dot_general(queries, keys, (((1,), (1,)), ((), ())), preferred_element_type=F32) * scale
            scores = jnp.where(allowed, scores, NEG)
            top = jnp.max(scores, axis=1, keepdims=True)
            probs = jnp.where(allowed, jnp.exp(scores - top), 0.0)
            denom = jnp.sum(probs, axis=1, keepdims=True)
            mixed = jnp.dot(probs.astype(BF16), vals, preferred_element_type=F32)
            done.append((mixed / denom).astype(BF16))
        for d in range(n):
            cut[d] = jnp.concatenate(
                [
                    done[g][i * tok : (i + 1) * tok, d * width : (d + 1) * width]
                    for g in range(groups)
                    for i in range(per)
                ],
                axis=1,
            )
        abuf[x, z] = cut[z]

    def attention_sends():
        out = []
        for k in range(1, n):
            to = peer(z, k, n)
            out.append((cut.at[to], abuf.at[x, z], a_s.at[k - 1], a_r.at[z], {"seq": to}))
        for j in range(1, m):
            out.append((cut.at[z], abuf.at[x, z], af_s.at[j - 1, z], af_r.at[j - 1, z], {"head": peer(x, j, m)}))
        return out

    def attention_at(cond):
        @pl.when(cond)
        def _():
            for s in range(n):
                @pl.when(s < z)
                def _(s=s):
                    arrived(kvbuf.at[s], kv_r.at[s], {"seq": s})

            attend()
            for item in attention_sends():
                remote(*item).start()

    def forward(b):
        @pl.when(z != b)
        def _():
            arrived(abuf.at[x, b], a_r.at[b], {"seq": b})
            for j in range(1, m):
                remote(
                    abuf.at[x, b], abuf.at[x, b], af_s.at[j - 1, b], af_r.at[j - 1, b], {"head": peer(x, j, m)}
                ).start()

    def a_ready(b):
        for j in range(1, m):
            h = source(x, j, m)
            arrived(abuf.at[h, b], af_r.at[j - 1, b], {"head": h})

    def project(b, c):
        cols = slice(c * cw, (c + 1) * cw)
        total = res_ref[:, cols].astype(F32) * (z == b).astype(F32)
        for h in range(m):
            total = total + jnp.dot(abuf[h, b], wbuf[h, c], preferred_element_type=F32)
        pbuf[b, c] = total

    def to_inner(b, c):
        pl.when(middle)(lambda: remote(sbuf.at[b, c], cross.at[b, c], s_s.at[b, c], c_r.at[b, c], {"seq": inner}).start())
        if n > 2:
            pl.when(jnp.logical_not(middle))(
                lambda: remote(sbuf.at[b, c], up.at[b, c], s_s.at[b, c], s_r.at[b, c], {"seq": inner}).start()
            )

    def first(b, c):
        sbuf[b, c] = pbuf[b, c].astype(BF16)
        to_inner(b, c)

    def inwards(b, c):
        arrived(up.at[b, c], s_r.at[b, c], {"seq": outer})
        sbuf[b, c] = (pbuf[b, c] + up[b, c].astype(F32)).astype(BF16)
        to_inner(b, c)

    def outwards(b, c):
        mine = st.at[x, c, b]

        @pl.when(middle)
        def _():
            arrived(cross.at[b, c], c_r.at[b, c], {"seq": inner})
            st[x, c, b] = (sbuf[b, c].astype(F32) + cross[b, c].astype(F32)).astype(BF16)

        if n > 2:
            @pl.when(jnp.logical_not(middle))
            def _():
                arrived(mine, t_r.at[b, c], {"seq": inner})

            @pl.when(has_outer)
            def _():
                remote(mine, mine, t_s.at[b, c], t_r.at[b, c], {"seq": outer}).start()
        for j in range(1, m):
            remote(mine, mine, x_s.at[j - 1, b, c], x_r.at[j - 1, b, c], {"head": peer(x, j, m)}).start()

    def routing():
        for s in range(n):
            @pl.when(s != z)
            def _(s=s):
                arrived(metas.at[s], me_r.at[s], {"seq": s})
        r_id = lax.broadcasted_iota(jnp.int32, (span, span), 0)
        c_id = lax.broadcasted_iota(jnp.int32, (span, span), 1)
        before = ((r_id < c_id) & (r_id // tok == c_id // tok)).astype(BF16)
        slot_id = lax.broadcasted_iota(jnp.int32, (part_slots, span), 0)
        base = (lax.broadcasted_iota(jnp.int32, (1, span), 1) // tok) * MOST
        for b in range(n // batch):
            meta = jnp.concatenate([metas[b * batch + i] for i in range(batch)], axis=1)
            weight = meta[2:3] / 256.0
            for e in range(experts):
                this = (x * experts + e).astype(F32)
                gate = jnp.where(meta[0:1] == this, weight, 0.0) + jnp.where(meta[1:2] == this, 1.0 - weight, 0.0)
                marked = gate > 0
                spread = jnp.broadcast_to(jnp.where(marked, 1.0, 0.0), (8, span)).astype(BF16)
                rank = jnp.dot(spread, before, preferred_element_type=F32)[0:1].astype(jnp.int32)
                pick = jnp.where(slot_id == jnp.where(marked, rank + base, -1), 1.0, 0.0)
                picks[b, e * part_slots : (e + 1) * part_slots] = pick.astype(BF16)
                gates[e, b * part_slots : (b + 1) * part_slots] = jnp.sum(pick * gate, axis=1, keepdims=True)

    def gather(c):
        for b in range(n):
            for j in range(1, m):
                h = source(x, j, m)
                arrived(st.at[h, c, b], x_r.at[j - 1, b, c], {"head": h})
        for h in range(m):
            start = h * share + c * cw
            gain = gain_ref[start : start + cw].astype(F32).reshape(1, cw)
            for b in range(n // batch):
                block = st[h, c, b * batch : (b + 1) * batch].reshape(span, cw)
                raw = jnp.dot(picks[b], block, preferred_element_type=F32)
                square = raw * raw
                folded = square[:, 0:128]
                for i in range(1, cw // 128):
                    folded = folded + square[:, i * 128 : (i + 1) * 128]
                scaled = (raw * gain).astype(BF16)
                own = slice(b * part_slots, (b + 1) * part_slots)
                for e in range(experts):
                    mine = slice(e * part_slots, (e + 1) * part_slots)
                    rows[e, own, h * cw : (h + 1) * cw] = scaled[mine]
                    if c == 0 and h == 0:
                        sq[e, own] = folded[mine]
                    else:
                        sq[e, own] += folded[mine]

    def in_batches(f):
        if n == batch:
            f(slice(None))
        else:
            pl.loop(0, n // batch)(lambda b: f(pl.ds(pl.multiple_of(b * part_slots, part_slots), part_slots)))

    def tile_of(c, e, u):
        return (c * experts + e) * 2 + u

    def multiply(c, e, u):
        q = tile_of(c, e, u)
        for copy in tile_copies(q):
            copy.wait()
        @in_batches
        def _(own):
            term = jnp.dot(rows[e, own], tiles[q % ring], preferred_element_type=F32)
            acc[e, u, own] = term if c == 0 else acc[e, u, own] + term
        if q + ring < len(order):
            for copy in tile_copies(q + ring):
                copy.start(priority=1)

    def finish(c, e):
        for u in range(2):
            for copy in tile_copies(tile_of(c, e, u)):
                copy.wait()
        step = min(hidden, 512)

        @in_batches
        def _(own):
            factor = lax.rsqrt(jnp.sum(sq[e, own], axis=1, keepdims=True) / (m * share) + EPS)
            for t in range(hidden // step):
                cols = slice(t * step, (t + 1) * step)
                part = []
                for u in range(2):
                    term = jnp.dot(rows[e, own], tiles[tile_of(c, e, u) % ring, :, cols], preferred_element_type=F32)
                    part.append((term if c == 0 else acc[e, u, own, cols] + term) * factor)
                act = part[0] / (1.0 + jnp.exp(-part[0]))
                hid[e, own, cols] = (gates[e, own] * (act * part[1])).astype(BF16)

        copy = pltpu.make_async_copy(hid.at[e], out_ref.at[e, 0], out_s.at[e])
        copy.start()
        return copy

    units = unit_order(n, parts)
    total_units = len(units)
    late = max(n - 2, 0) * parts
    at_end = jnp.logical_not(has_outer)

    def of_block(b):
        return [(b, c) for c in range(parts)]

    def run(cond, events):
        if events:
            @pl.when(cond)
            def _():
                for f, u in events:
                    f(*u)

    def start_sum(b, c):
        if b < n - 2:
            run(at_end, [(first, (b, c))])
        elif c == parts - 1:
            early = early_of(parts)
            run(at_end, [(first, u) for u in ([(b, i) for i in range(early)] if b == n - 2 else units[late + early :])])

    def stage(b):
        a_ready(b)
        for c in range(parts):
            project(b, c)
            start_sum(b, c)

    attention_at(z == 0)
    over_x = [functools.partial(w_over_x, c) for c in range(parts)]
    over_x.pop(0)()
    forward(0)
    attention_at(z == 1)
    for _ in range(min(3, len(over_x))):
        over_x.pop(0)()
    if n > 2:
        attention_at(z >= 2)
    later = [functools.partial(forward, b) for b in range(1, n)]
    for c in range(parts):
        if over_x:
            over_x.pop(0)()
        w_over_y(c)
        w_ready(c)
        if c == 0:
            a_ready(0)
        project(0, c)
        start_sum(0, c)
        if c % 2 == 1 and len(later) > 1:
            later.pop(0)()
    for f in later:
        f()
    routing()
    for b in range(1, n):
        events = []
        for i in range(parts):
            if b >= 3:
                events.append((outwards, of_block(b - 3)[i]))
            if b >= 2:
                events.append((inwards, of_block(b - 2)[i]))
        run(has_outer, events)
        stage(b)

    run(at_end, [(outwards, u) for u in units[:late]])
    events = []
    for i in range(parts):
        if n >= 3:
            events.append((outwards, of_block(n - 3)[i]))
            events.append((inwards, units[late + i]))
    run(has_outer, events)
    ready = [max(i for i, u in enumerate(units) if u[1] == c) for c in range(parts)]
    work = []
    for c in range(parts - 1):
        work.append((ready[c] + 2, functools.partial(gather, c)))
        for e in range(experts):
            work.append((ready[c] + 2, functools.partial(multiply, c, e, 0)))
            work.append((ready[c] + 2, functools.partial(multiply, c, e, 1)))
    for j in range(late, total_units):
        if j + parts < total_units and n >= 3:
            run(has_outer, [(inwards, units[j + parts])])
        outwards(*units[j])
        for _ in range(2):
            if work and work[0][0] <= j:
                work.pop(0)[1]()
    for _, f in work:
        f()
    gather(parts - 1)
    outs = []
    for c in range(parts):
        outs.append(pltpu.make_async_copy(st.at[x, c, z], own_ref.at[:, pl.ds(c * cw, cw)], out_s.at[experts + c]))
        outs[-1].start()
    for e in range(experts):
        outs.append(finish(parts - 1, e))

    for cond, make in sends:
        if cond is None:
            make().wait_send()
        else:
            pl.when(cond)(lambda make=make: make().wait_send())

    for item in attention_sends():
        remote(*item).wait_send()
    for b in range(n):
        @pl.when(z != b)
        def _(b=b):
            for j in range(1, m):
                remote(
                    abuf.at[x, b], abuf.at[x, b], af_s.at[j - 1, b], af_r.at[j - 1, b], {"head": peer(x, j, m)}
                ).wait_send()
    for b, c in units:
        remote(sbuf.at[b, c], cross.at[b, c], s_s.at[b, c], c_r.at[b, c], {"seq": inner}).wait_send()
        mine = st.at[x, c, b]
        if n > 2:
            @pl.when(has_outer)
            def _(b=b, c=c, mine=mine):
                remote(mine, mine, t_s.at[b, c], t_r.at[b, c], {"seq": outer}).wait_send()
        for j in range(1, m):
            remote(mine, mine, x_s.at[j - 1, b, c], x_r.at[j - 1, b, c], {"head": peer(x, j, m)}).wait_send()
    for copy in outs:
        copy.wait()


def place_kernel(own_ref, hidden_ref, own_out, hidden_out, sems):
    first = pltpu.make_async_copy(own_ref, own_out, sems.at[0])
    second = pltpu.make_async_copy(hidden_ref, hidden_out, sems.at[1])
    first.start()
    second.start()
    first.wait()
    second.wait()


def local(
    n, m, nd, ng,
    queries, keys, values, residual_in, out_proj, norm_gain,
    expert_gate, expert_up, routes, gate_numer, sequence_lengths,
):
    tok, feats = queries.shape[1:]
    kv = keys.shape[2]
    share = residual_in.shape[2]
    heads, width, features = out_proj.shape
    depth = heads * width
    experts, _, hidden = expert_gate.shape
    slots = n * MOST
    batch = 4 if n % 4 == 0 else n
    parts = max(p for p in range(1, share // 128 + 1) if share % (128 * p) == 0 and (p == 1 or n * p <= UNITS))
    cw = share // parts
    pieces = ng * nd if depth % (16 * ng * nd) == 0 else 1
    ring = min(2 * parts * experts, RING_BYTES // (2 * m * cw * hidden))
    vmem = pl.BlockSpec(memory_space=pltpu.VMEM)
    hbm = pl.BlockSpec(memory_space=pl.ANY)
    dma = pltpu.SemaphoreType.DMA
    own, hidden_out = pl.pallas_call(
        functools.partial(mix_kernel, n, m, nd, ng, pieces),
        out_shape=(
            jax.ShapeDtypeStruct((tok, share), BF16),
            jax.ShapeDtypeStruct((experts, 1, slots, hidden), BF16),
        ),
        in_specs=[pl.BlockSpec(memory_space=pltpu.SMEM)] + [hbm] * 10,
        out_specs=(hbm, hbm),
        scratch_shapes=[
            pltpu.VMEM((tok, feats), BF16),
            pltpu.VMEM((2, tok), jnp.int32),
            pltpu.VMEM((1, tok), jnp.int32),
            pltpu.VMEM((tok, share), BF16),
            pltpu.VMEM((features,), BF16),
            pltpu.VMEM((m, parts, n, tok, cw), BF16),
            pltpu.VMEM((n, 8, tok), F32),
            pltpu.VMEM((8, tok), F32),
            pltpu.VMEM((ring, m * cw, hidden), BF16),
            pltpu.VMEM((experts, 2, slots, hidden), F32),
            pltpu.VMEM((experts, slots, m * cw), BF16),
            pltpu.VMEM((experts, slots, 128), F32),
            pltpu.VMEM((n // batch, experts * batch * MOST, batch * tok), BF16),
            pltpu.VMEM((experts, slots, 1), F32),
            pltpu.VMEM((n, tok, 2 * kv), BF16),
            pltpu.VMEM((m, parts, depth, cw), BF16),
            pltpu.VMEM((n, tok, depth), BF16),
            pltpu.VMEM((m, n, tok, depth), BF16),
            pltpu.VMEM((n, parts, tok, cw), F32),
            pltpu.VMEM((n, parts, tok, cw), BF16),
            pltpu.VMEM((n, parts, tok, cw), BF16),
            pltpu.VMEM((n, parts, tok, cw), BF16),
            pltpu.VMEM((experts, slots, hidden), BF16),
            dma((7,)),
            dma((n - 1,)), dma((n,)),
            dma((n - 1,)), dma((n,)),
            dma((m - 1, parts)), dma((m - 1, parts)),
            dma((m - 1, parts, max(ng - 1, 1))), dma((m - 1, parts, max(ng - 1, 1))),
            dma((m - 1, parts, max(nd - 1, 1), ng)), dma((m - 1, parts, max(nd - 1, 1), ng)),
            dma((parts,)),
            dma((n - 1,)), dma((n,)), dma((m - 1, n)), dma((m - 1, n)),
            dma((n, parts)), dma((n, parts)), dma((n, parts)),
            dma((n, parts)), dma((n, parts)),
            dma((m - 1, n, parts)), dma((m - 1, n, parts)),
            dma((ring, m)), dma((experts + parts,)),
        ],
        compiler_params=pltpu.CompilerParams(
            collective_id=0, has_side_effects=True, vmem_limit_bytes=63 * 1024 * 1024
        ),
    )(
        sequence_lengths, queries[0], keys[0], values[0], routes[0].T, gate_numer, residual_in[0],
        norm_gain, out_proj.reshape(depth, features), expert_gate, expert_up,
    )
    own, hidden_out = pl.pallas_call(
        place_kernel,
        out_shape=tuple(jax.ShapeDtypeStruct(a.shape, a.dtype) for a in (own, hidden_out)),
        in_specs=[vmem, vmem],
        out_specs=(hbm, hbm),
        scratch_shapes=[dma((2,))],
    )(own, hidden_out)
    return (own[None], hidden_out)


def solution(mesh):
    seq_spec = P(("grp", "dat"), "seq", "head")
    in_specs = (
        seq_spec, seq_spec, seq_spec, seq_spec,
        P("head", "seq", None), P(),
        P("head", None, "seq"), P("head", None, "seq"),
        P(("grp", "dat"), "seq", None), P(("grp", "dat"), "seq"), P(("grp", "dat")),
    )
    out_specs = (seq_spec, P("head", ("grp", "dat"), None, "seq"))
    sizes = [mesh.shape[axis] for axis in ("seq", "head", "dat", "grp")]
    body = functools.partial(local, *sizes)
    return jax.shard_map(body, mesh=mesh, in_specs=in_specs, out_specs=out_specs, check_vma=False)
```

```python
import functools
import math

import jax
import jax.numpy as jnp
from jax import lax
from jax.experimental import pallas as pl
from jax.experimental.pallas import tpu as pltpu
from jax.sharding import PartitionSpec as P

HEAD_SIZE = 128
MOST = 40
EPS = 1e-05
NEG = -1e30
RING_BYTES = 36 * 1024 * 1024
UNITS = 16
LAG = 2
PIECES = 2
MESH = pl.DeviceIdType.MESH
F32 = jnp.float32
BF16 = jnp.bfloat16


def groups_of(n, parts, b):
    if parts % 2 or parts < 6:
        return [(c, 1) for c in range(parts)]
    if b == n - 1:
        return [(0, 1), (1, 1)] + [(c, 2) for c in range(2, parts, 2)]
    return [(c, 2) for c in range(0, parts, 2)]


def unit_order(n, parts):
    blocks = [[(b, *g) for g in groups_of(n, parts, b)] for b in range(n)]
    units = [u for b in range(max(n - 2, 0)) for u in blocks[b]]
    late = len(units)
    units += blocks[n - 2][:1]
    last = len(units)
    units += blocks[n - 1][:1]
    for pair in zip(blocks[n - 2][1:], blocks[n - 1][1:]):
        units += pair
    return units, late, last


def mix_kernel(
    n, m, nd, ng, pieces,
    len_ref, q_hbm, k_hbm, v_hbm, route_hbm, numer_hbm, res_hbm, gain_hbm, w_ref, wg_ref, wu_ref,
    own_ref, out_ref,
    q_ref, route_ref, numer_ref, res_ref, gain_ref,
    st, metas, meta_ref, tiles, acc, rows, sq, picks, gates,
    kvbuf, wbuf, cut, abuf, pbuf, sbuf, up, cross, hid,
    in_s, kv_s, kv_r, me_s, me_r, w_s, w_r, wy_s, wy_r, wd_s, wd_r, wl,
    a_s, a_r, af_s, af_r, s_s, s_r, c_r, t_s, t_r, x_s, x_r, tile_s, out_s,
):
    z = lax.axis_index("seq")
    x = lax.axis_index("head")
    c_me = lax.axis_index("dat")
    g_me = lax.axis_index("grp")
    tok, share = res_ref.shape
    heads = q_ref.shape[1] // HEAD_SIZE
    kv = kvbuf.shape[2] // 2
    groups = kv // HEAD_SIZE
    per = heads // groups
    width = HEAD_SIZE // n
    parts, cw = st.shape[2], st.shape[4]
    depth = abuf.shape[3]
    cuts = 2 if parts % 2 == 0 else 1
    ww = share // cuts
    experts, hidden = acc.shape[0], acc.shape[3]
    ring = tiles.shape[0]
    half = n // 2
    batch = 4 if n % 4 == 0 else n
    span, part_slots = batch * tok, batch * MOST

    lower = z < half
    inner = jnp.where(lower, z + 1, z - 1)
    outer = jnp.where(lower, z - 1, z + 1)
    middle = (z == half - 1) | (z == half)
    has_outer = (z > 0) & (z < n - 1)

    def peer(me, k, size):
        return lax.rem(me + k, size)

    def source(me, k, size):
        return lax.rem(me - k + size, size)

    sends = []

    def remote(src, dst, s_sem, r_sem, where):
        return pltpu.make_async_remote_copy(
            src_ref=src, dst_ref=dst, send_sem=s_sem, recv_sem=r_sem,
            device_id=where, device_id_type=MESH,
        )

    def send(src, dst, s_sem, r_sem, where, cond=None):
        make = functools.partial(remote, src, dst, s_sem, r_sem, where)
        if cond is None:
            make().start()
        else:
            pl.when(cond)(lambda: make().start())
        sends.append((cond, make))

    def arrived(dst, r_sem, where):
        remote(dst, dst, in_s.at[0], r_sem, where).wait_recv()

    order = [(c, e, u) for c in range(parts) for e in range(experts) for u in range(2)]

    def tile_copies(q):
        c, e, u = order[q]
        return [
            pltpu.make_async_copy(
                (wg_ref, wu_ref)[u].at[e, pl.ds(h * share + c * cw, cw), :],
                tiles.at[q % ring, pl.ds(h * cw, cw), :],
                tile_s.at[q % ring, h],
            )
            for h in range(m)
        ]

    barrier = pltpu.get_barrier_semaphore()
    count = 0
    for axis, me, size in (("seq", z, n), ("head", x, m), ("dat", c_me, nd), ("grp", g_me, ng)):
        for k in range(1, size):
            pl.semaphore_signal(barrier, inc=1, device_id={axis: peer(me, k, size)}, device_id_type=MESH)
            count += 1
    loads = [
        pltpu.make_async_copy(src, dst, in_s.at[i])
        for i, (src, dst) in enumerate((
            (k_hbm, kvbuf.at[z, :, pl.ds(0, kv)]), (v_hbm, kvbuf.at[z, :, pl.ds(kv, kv)]), (q_hbm, q_ref),
            (route_hbm, route_ref), (numer_hbm, numer_ref), (res_hbm, res_ref), (gain_hbm, gain_ref),
        ))
    ]
    for load in loads:
        load.start()
    own_w = []
    for c in range(cuts):
        start = pl.multiple_of(x * share + c * ww, 128)
        own_w.append(pltpu.make_async_copy(
            w_ref.at[:, pl.ds(start, ww)], wbuf.at[x, :, pl.ds(c * ww, ww)], wl.at[c]
        ))
        own_w[-1].start()
    for q in range(min(ring, len(order))):
        for copy in tile_copies(q):
            copy.start(priority=1)
    for s in range(n):
        @pl.when(s > z)
        def _(s=s):
            kvbuf[s] = jnp.zeros(kvbuf.shape[1:], BF16)
    for load in loads:
        load.wait()
    meta_ref[0:2] = route_ref[...].astype(F32)
    meta_ref[2:3] = numer_ref[...].astype(F32)
    meta_ref[3:8] = jnp.zeros((5, tok), F32)
    metas[z] = meta_ref[...]
    pl.semaphore_wait(barrier, count)

    for k in range(n - 1, 0, -1):
        to = jnp.minimum(z + k, n - 1)
        send(kvbuf.at[z], kvbuf.at[z], kv_s.at[k - 1], kv_r.at[z], {"seq": to}, z + k < n)
    w_rows = depth // pieces
    piece = g_me * nd + c_me if pieces > 1 else 0

    def w_block(h, c, p):
        return wbuf.at[h, pl.ds(pl.multiple_of(p * w_rows, w_rows), w_rows), pl.ds(c * ww, ww)]

    for c in range(cuts):
        for j in range(1, m):
            to = peer(x, j, m)
            start = pl.multiple_of(to * share + c * ww, 128)
            src = w_ref.at[pl.ds(pl.multiple_of(piece * w_rows, w_rows), w_rows), pl.ds(start, ww)]
            send(src, w_block(x, c, piece), w_s.at[j - 1, c], w_r.at[j - 1, c], {"head": to})
    for k in range(1, n):
        send(meta_ref, metas.at[z], me_s.at[k - 1], me_r.at[z], {"seq": peer(z, k, n)})

    def w_over_x(c):
        for j in range(1, m):
            s = source(x, j, m)
            block = w_block(s, c, piece)
            arrived(block, w_r.at[j - 1, c], {"head": s})
            if pieces > 1:
                for k in range(1, ng):
                    send(block, block, wy_s.at[j - 1, c, k - 1], wy_r.at[j - 1, c, k - 1], {"grp": peer(g_me, k, ng)})
                for i in range(1, nd):
                    send(block, block, wd_s.at[j - 1, c, i - 1, 0], wd_r.at[j - 1, c, i - 1, 0], {"dat": peer(c_me, i, nd)})

    def w_over_y(c):
        if pieces == 1:
            return
        for j in range(1, m):
            s = source(x, j, m)
            for k in range(1, ng):
                g = source(g_me, k, ng)
                block = w_block(s, c, g * nd + c_me)
                arrived(block, wy_r.at[j - 1, c, k - 1], {"grp": g})
                for i in range(1, nd):
                    send(block, block, wd_s.at[j - 1, c, i - 1, k], wd_r.at[j - 1, c, i - 1, k], {"dat": peer(c_me, i, nd)})

    def w_ready(c):
        own_w[c].wait()
        if pieces == 1:
            return
        for j in range(1, m):
            s = source(x, j, m)
            for i in range(1, nd):
                d = source(c_me, i, nd)
                for k in range(ng):
                    g = source(g_me, k, ng)
                    arrived(w_block(s, c, g * nd + d), wd_r.at[j - 1, c, i - 1, k], {"dat": d})

    def attend():
        row = lax.broadcasted_iota(jnp.int32, (per * tok, n * tok), 0)
        col = lax.broadcasted_iota(jnp.int32, (per * tok, n * tok), 1)
        allowed = (col <= lax.rem(row, tok) + z * tok) & (col < len_ref[0])
        scale = 1.0 / math.sqrt(HEAD_SIZE)
        done = []
        for g in range(groups):
            lanes = slice(g * HEAD_SIZE, (g + 1) * HEAD_SIZE)
            queries = jnp.concatenate(
                [q_ref[:, (g * per + i) * HEAD_SIZE : (g * per + i + 1) * HEAD_SIZE] for i in range(per)], axis=0
            )
            keys = kvbuf[:, :, lanes].reshape(n * tok, HEAD_SIZE)
            vals = kvbuf[:, :, kv + g * HEAD_SIZE : kv + (g + 1) * HEAD_SIZE].reshape(n * tok, HEAD_SIZE)
            scores = lax.dot_general(queries, keys, (((1,), (1,)), ((), ())), preferred_element_type=F32) * scale
            scores = jnp.where(allowed, scores, NEG)
            top = jnp.max(scores, axis=1, keepdims=True)
            probs = jnp.where(allowed, jnp.exp(scores - top), 0.0)
            denom = jnp.sum(probs, axis=1, keepdims=True)
            mixed = jnp.dot(probs.astype(BF16), vals, preferred_element_type=F32)
            done.append((mixed / denom).astype(BF16))
        for d in range(n):
            cut[d] = jnp.concatenate(
                [
                    done[g][i * tok : (i + 1) * tok, d * width : (d + 1) * width]
                    for g in range(groups)
                    for i in range(per)
                ],
                axis=1,
            )
        abuf[x, z] = cut[z]

    def attention_sends():
        out = []
        for k in range(1, n):
            to = peer(z, k, n)
            out.append((cut.at[to], abuf.at[x, z], a_s.at[k - 1], a_r.at[z], {"seq": to}))
        for j in range(1, m):
            out.append((cut.at[z], abuf.at[x, z], af_s.at[j - 1, z], af_r.at[j - 1, z], {"head": peer(x, j, m)}))
        return out

    def attention_at(cond):
        @pl.when(cond)
        def _():
            for s in range(n):
                @pl.when(s < z)
                def _(s=s):
                    arrived(kvbuf.at[s], kv_r.at[s], {"seq": s})

            attend()
            for item in attention_sends():
                remote(*item).start()

    def forward(b):
        @pl.when(z != b)
        def _():
            arrived(abuf.at[x, b], a_r.at[b], {"seq": b})
            for j in range(1, m):
                remote(
                    abuf.at[x, b], abuf.at[x, b], af_s.at[j - 1, b], af_r.at[j - 1, b], {"head": peer(x, j, m)}
                ).start()

    def a_ready(b):
        for j in range(1, m):
            h = source(x, j, m)
            arrived(abuf.at[h, b], af_r.at[j - 1, b], {"head": h})

    def project(b, c, k):
        cols = slice(c * cw, (c + k) * cw)
        total = res_ref[:, cols].astype(F32) * (z == b).astype(F32)
        for h in range(m):
            total = total + jnp.dot(abuf[h, b], wbuf[h, :, cols], preferred_element_type=F32)
        for i in range(k):
            pbuf[b, c + i] = total[:, i * cw : (i + 1) * cw]

    def to_inner(b, c, k):
        def start(dst, r_sem):
            remote(sbuf.at[b, pl.ds(c, k)], dst.at[b, pl.ds(c, k)], s_s.at[b, c], r_sem.at[b, c], {"seq": inner}).start()

        pl.when(middle)(lambda: start(cross, c_r))
        if n > 2:
            pl.when(jnp.logical_not(middle))(lambda: start(up, s_r))

    def first(b, c, k):
        sbuf[b, c : c + k] = pbuf[b, c : c + k].astype(BF16)
        to_inner(b, c, k)

    def inwards(b, c, k):
        own = slice(c, c + k)
        arrived(up.at[b, pl.ds(c, k)], s_r.at[b, c], {"seq": outer})
        sbuf[b, own] = (pbuf[b, own] + up[b, own].astype(F32)).astype(BF16)
        to_inner(b, c, k)

    def outwards(b, c, k):
        mine = st.at[x, b, pl.ds(c, k)]
        own = slice(c, c + k)

        @pl.when(middle)
        def _():
            arrived(cross.at[b, pl.ds(c, k)], c_r.at[b, c], {"seq": inner})
            st[x, b, own] = (sbuf[b, own].astype(F32) + cross[b, own].astype(F32)).astype(BF16)

        if n > 2:
            @pl.when(jnp.logical_not(middle))
            def _():
                arrived(mine, t_r.at[b, c], {"seq": inner})

            @pl.when(has_outer)
            def _():
                remote(mine, mine, t_s.at[b, c], t_r.at[b, c], {"seq": outer}).start()
        for j in range(1, m):
            remote(mine, mine, x_s.at[j - 1, b, c], x_r.at[j - 1, b, c], {"head": peer(x, j, m)}).start()

    def routing():
        for s in range(n):
            @pl.when(s != z)
            def _(s=s):
                arrived(metas.at[s], me_r.at[s], {"seq": s})
        r_id = lax.broadcasted_iota(jnp.int32, (span, span), 0)
        c_id = lax.broadcasted_iota(jnp.int32, (span, span), 1)
        before = ((r_id < c_id) & (r_id // tok == c_id // tok)).astype(BF16)
        slot_id = lax.broadcasted_iota(jnp.int32, (part_slots, span), 0)
        base = (lax.broadcasted_iota(jnp.int32, (1, span), 1) // tok) * MOST
        for b in range(n // batch):
            meta = jnp.concatenate([metas[b * batch + i] for i in range(batch)], axis=1)
            weight = meta[2:3] / 256.0
            for e in range(experts):
                this = (x * experts + e).astype(F32)
                gate = jnp.where(meta[0:1] == this, weight, 0.0) + jnp.where(meta[1:2] == this, 1.0 - weight, 0.0)
                marked = gate > 0
                spread = jnp.broadcast_to(jnp.where(marked, 1.0, 0.0), (8, span)).astype(BF16)
                rank = jnp.dot(spread, before, preferred_element_type=F32)[0:1].astype(jnp.int32)
                pick = jnp.where(slot_id == jnp.where(marked, rank + base, -1), 1.0, 0.0)
                picks[b, e * part_slots : (e + 1) * part_slots] = pick.astype(BF16)
                gates[e, b * part_slots : (b + 1) * part_slots] = jnp.sum(pick * gate, axis=1, keepdims=True)

    def gather(c):
        for b, first_c, k in units:
            if first_c == c:
                for j in range(1, m):
                    h = source(x, j, m)
                    arrived(st.at[h, b, pl.ds(c, k)], x_r.at[j - 1, b, c], {"head": h})
        for h in range(m):
            start = h * share + c * cw
            gain = gain_ref[start : start + cw].astype(F32).reshape(1, cw)
            for b in range(n // batch):
                block = st[h, b * batch : (b + 1) * batch, c].reshape(span, cw)
                raw = jnp.dot(picks[b], block, preferred_element_type=F32)
                square = raw * raw
                folded = square[:, 0:128]
                for i in range(1, cw // 128):
                    folded = folded + square[:, i * 128 : (i + 1) * 128]
                scaled = (raw * gain).astype(BF16)
                own = slice(b * part_slots, (b + 1) * part_slots)
                for e in range(experts):
                    mine = slice(e * part_slots, (e + 1) * part_slots)
                    rows[e, own, h * cw : (h + 1) * cw] = scaled[mine]
                    if c == 0 and h == 0:
                        sq[e, own] = folded[mine]
                    else:
                        sq[e, own] += folded[mine]

    def in_batches(f):
        if n == batch:
            f(slice(None))
        else:
            pl.loop(0, n // batch)(lambda b: f(pl.ds(pl.multiple_of(b * part_slots, part_slots), part_slots)))

    def tile_of(c, e, u):
        return (c * experts + e) * 2 + u

    def multiply(c, e, u):
        q = tile_of(c, e, u)
        for copy in tile_copies(q):
            copy.wait()
        @in_batches
        def _(own):
            term = jnp.dot(rows[e, own], tiles[q % ring], preferred_element_type=F32)
            acc[e, u, own] = term if c == 0 else acc[e, u, own] + term
        if q + ring < len(order):
            for copy in tile_copies(q + ring):
                copy.start(priority=1)

    def finish(c, e):
        for u in range(2):
            for copy in tile_copies(tile_of(c, e, u)):
                copy.wait()
        step = min(hidden, 512)

        @in_batches
        def _(own):
            factor = lax.rsqrt(jnp.sum(sq[e, own], axis=1, keepdims=True) / (m * share) + EPS)
            for t in range(hidden // step):
                cols = slice(t * step, (t + 1) * step)
                part = []
                for u in range(2):
                    term = jnp.dot(rows[e, own], tiles[tile_of(c, e, u) % ring, :, cols], preferred_element_type=F32)
                    part.append((term if c == 0 else acc[e, u, own, cols] + term) * factor)
                act = part[0] / (1.0 + jnp.exp(-part[0]))
                hid[e, own, cols] = (gates[e, own] * (act * part[1])).astype(BF16)

        copy = pltpu.make_async_copy(hid.at[e], out_ref.at[e, 0], out_s.at[e])
        copy.start()
        return copy

    units, late, last = unit_order(n, parts)
    at_end = jnp.logical_not(has_outer)

    def of_block(b):
        return [u for u in units if u[0] == b]

    def run(cond, events):
        if events:
            @pl.when(cond)
            def _():
                for f, u in events:
                    f(*u)

    def start_sum(b, c):
        if b < n - 1:
            run(at_end, [(first, u) for u in units[:last] if u[0] == b and u[1] + u[2] - 1 == c])
        elif c == parts - 1:
            run(at_end, [(first, u) for u in units[last:]])

    def stage(b):
        a_ready(b)
        project(b, 0, parts)
        for c in range(parts):
            start_sum(b, c)

    attention_at(z == 0)
    over_x = [functools.partial(w_over_x, c) for c in range(cuts)]
    over_x.pop(0)()
    forward(0)
    attention_at(z == 1)
    for f in over_x[:1]:
        f()
    if n > 2:
        attention_at(z >= 2)
    for f in over_x[1:]:
        f()
    later = [functools.partial(forward, b) for b in range(1, n)]
    for c in range(cuts):
        w_over_y(c)
        w_ready(c)
        if c == 0:
            a_ready(0)
        project(0, c * (parts // cuts), parts // cuts)
        for i in range(c * (parts // cuts), (c + 1) * (parts // cuts)):
            start_sum(0, i)
        if len(later) > 1:
            later.pop(0)()
    for f in later:
        f()
    for b in range(1, n):
        events = []
        for i in range(parts):
            if b >= 3:
                events += [(outwards, u) for u in of_block(b - 3)[i : i + 1]]
            if b >= 2:
                events += [(inwards, u) for u in of_block(b - 2)[i : i + 1]]
        run(has_outer, events)
        stage(b)
    routing()

    run(at_end, [(outwards, u) for u in units[:late]])
    todo = units[late:]
    if n >= 3:
        events = []
        for u in of_block(n - 3):
            events += [(outwards, u)] + [(inwards, v) for v in todo[:1]]
            todo = todo[1:]
        run(has_outer, events)
    else:
        todo = []
    ready = [max(i for i, u in enumerate(units) if u[1] <= c < u[1] + u[2]) for c in range(parts)]
    work = []
    for c in range(parts - 1):
        work.append((ready[c] + LAG, functools.partial(gather, c)))
        for e in range(experts):
            work.append((ready[c] + LAG, functools.partial(multiply, c, e, 0)))
            work.append((ready[c] + LAG, functools.partial(multiply, c, e, 1)))
    for j in range(late, len(units)):
        run(has_outer, [(inwards, v) for v in todo[:1]])
        todo = todo[1:]
        outwards(*units[j])
        for _ in range(PIECES):
            if work and work[0][0] <= j:
                work.pop(0)[1]()
    for _, f in work:
        f()
    gather(parts - 1)
    outs = []
    for c in range(parts):
        outs.append(pltpu.make_async_copy(st.at[x, z, c], own_ref.at[:, pl.ds(c * cw, cw)], out_s.at[experts + c]))
        outs[-1].start()
    for e in range(experts):
        outs.append(finish(parts - 1, e))

    for cond, make in sends:
        if cond is None:
            make().wait_send()
        else:
            pl.when(cond)(lambda make=make: make().wait_send())

    for item in attention_sends():
        remote(*item).wait_send()
    for b in range(n):
        @pl.when(z != b)
        def _(b=b):
            for j in range(1, m):
                remote(
                    abuf.at[x, b], abuf.at[x, b], af_s.at[j - 1, b], af_r.at[j - 1, b], {"head": peer(x, j, m)}
                ).wait_send()
    for b, c, k in units:
        own = sbuf.at[b, pl.ds(c, k)]
        remote(own, own, s_s.at[b, c], s_r.at[b, c], {"seq": inner}).wait_send()
        mine = st.at[x, b, pl.ds(c, k)]
        if n > 2:
            @pl.when(has_outer)
            def _(b=b, c=c, mine=mine):
                remote(mine, mine, t_s.at[b, c], t_r.at[b, c], {"seq": outer}).wait_send()
        for j in range(1, m):
            remote(mine, mine, x_s.at[j - 1, b, c], x_r.at[j - 1, b, c], {"head": peer(x, j, m)}).wait_send()
    for copy in outs:
        copy.wait()


def place_kernel(own_ref, hidden_ref, own_out, hidden_out, own_buf, hidden_buf, sems):
    experts = hidden_ref.shape[0]
    moves = [(own_ref, own_buf, own_out)]
    moves += [(hidden_ref.at[e], hidden_buf.at[e], hidden_out.at[e]) for e in range(experts)]
    loads = [pltpu.make_async_copy(src, buf, sems.at[0, i]) for i, (src, buf, _) in enumerate(moves)]
    stores = [pltpu.make_async_copy(buf, dst, sems.at[1, i]) for i, (_, buf, dst) in enumerate(moves)]
    for load in loads:
        load.start()
    for load, store in zip(loads, stores):
        load.wait()
        store.start()
    for store in stores:
        store.wait()


def local(
    n, m, nd, ng,
    queries, keys, values, residual_in, out_proj, norm_gain,
    expert_gate, expert_up, routes, gate_numer, sequence_lengths,
):
    tok, feats = queries.shape[1:]
    kv = keys.shape[2]
    share = residual_in.shape[2]
    heads, width, features = out_proj.shape
    depth = heads * width
    experts, _, hidden = expert_gate.shape
    slots = n * MOST
    batch = 4 if n % 4 == 0 else n
    parts = max(p for p in range(1, share // 128 + 1) if share % (128 * p) == 0 and (p == 1 or n * p <= UNITS))
    cw = share // parts
    pieces = ng * nd if depth % (16 * ng * nd) == 0 else 1
    ring = min(2 * parts * experts, RING_BYTES // (2 * m * cw * hidden))
    vmem = pl.BlockSpec(memory_space=pltpu.VMEM)
    hbm = pl.BlockSpec(memory_space=pl.ANY)
    dma = pltpu.SemaphoreType.DMA
    own, hidden_out = pl.pallas_call(
        functools.partial(mix_kernel, n, m, nd, ng, pieces),
        out_shape=(
            jax.ShapeDtypeStruct((tok, share), BF16),
            jax.ShapeDtypeStruct((experts, 1, slots, hidden), BF16),
        ),
        in_specs=[pl.BlockSpec(memory_space=pltpu.SMEM)] + [hbm] * 10,
        out_specs=(hbm, hbm),
        scratch_shapes=[
            pltpu.VMEM((tok, feats), BF16),
            pltpu.VMEM((2, tok), jnp.int32),
            pltpu.VMEM((1, tok), jnp.int32),
            pltpu.VMEM((tok, share), BF16),
            pltpu.VMEM((features,), BF16),
            pltpu.VMEM((m, n, parts, tok, cw), BF16),
            pltpu.VMEM((n, 8, tok), F32),
            pltpu.VMEM((8, tok), F32),
            pltpu.VMEM((ring, m * cw, hidden), BF16),
            pltpu.VMEM((experts, 2, slots, hidden), F32),
            pltpu.VMEM((experts, slots, m * cw), BF16),
            pltpu.VMEM((experts, slots, 128), F32),
            pltpu.VMEM((n // batch, experts * batch * MOST, batch * tok), BF16),
            pltpu.VMEM((experts, slots, 1), F32),
            pltpu.VMEM((n, tok, 2 * kv), BF16),
            pltpu.VMEM((m, depth, share), BF16),
            pltpu.VMEM((n, tok, depth), BF16),
            pltpu.VMEM((m, n, tok, depth), BF16),
            pltpu.VMEM((n, parts, tok, cw), F32),
            pltpu.VMEM((n, parts, tok, cw), BF16),
            pltpu.VMEM((n, parts, tok, cw), BF16),
            pltpu.VMEM((n, parts, tok, cw), BF16),
            pltpu.VMEM((experts, slots, hidden), BF16),
            dma((7,)),
            dma((n - 1,)), dma((n,)),
            dma((n - 1,)), dma((n,)),
            dma((m - 1, parts)), dma((m - 1, parts)),
            dma((m - 1, parts, max(ng - 1, 1))), dma((m - 1, parts, max(ng - 1, 1))),
            dma((m - 1, parts, max(nd - 1, 1), ng)), dma((m - 1, parts, max(nd - 1, 1), ng)),
            dma((parts,)),
            dma((n - 1,)), dma((n,)), dma((m - 1, n)), dma((m - 1, n)),
            dma((n, parts)), dma((n, parts)), dma((n, parts)),
            dma((n, parts)), dma((n, parts)),
            dma((m - 1, n, parts)), dma((m - 1, n, parts)),
            dma((ring, m)), dma((experts + parts,)),
        ],
        compiler_params=pltpu.CompilerParams(
            collective_id=0, has_side_effects=True, vmem_limit_bytes=63 * 1024 * 1024
        ),
    )(
        sequence_lengths, queries[0], keys[0], values[0], routes[0].T, gate_numer, residual_in[0],
        norm_gain, out_proj.reshape(depth, features), expert_gate, expert_up,
    )
    own, hidden_out = pl.pallas_call(
        place_kernel,
        out_shape=tuple(jax.ShapeDtypeStruct(a.shape, a.dtype) for a in (own, hidden_out)),
        in_specs=[hbm, hbm],
        out_specs=(hbm, hbm),
        scratch_shapes=[
            pltpu.VMEM(own.shape, BF16), pltpu.VMEM(hidden_out.shape, BF16), dma((2, 1 + experts)),
        ],
    )(own, hidden_out)
    return (own[None], hidden_out)


def solution(mesh):
    seq_spec = P(("grp", "dat"), "seq", "head")
    in_specs = (
        seq_spec, seq_spec, seq_spec, seq_spec,
        P("head", "seq", None), P(),
        P("head", None, "seq"), P("head", None, "seq"),
        P(("grp", "dat"), "seq", None), P(("grp", "dat"), "seq"), P(("grp", "dat")),
    )
    out_specs = (seq_spec, P("head", ("grp", "dat"), None, "seq"))
    sizes = [mesh.shape[axis] for axis in ("seq", "head", "dat", "grp")]
    body = functools.partial(local, *sizes)
    return jax.shard_map(body, mesh=mesh, in_specs=in_specs, out_specs=out_specs, check_vma=False)
```

```python
import functools
import math

import jax
import jax.numpy as jnp
from jax import lax
from jax.experimental import pallas as pl
from jax.experimental.pallas import tpu as pltpu
from jax.sharding import PartitionSpec as P

HEAD_SIZE = 128
MOST = 40
EPS = 1e-05
NEG = -1e30
RING_BYTES = 36 * 1024 * 1024
UNITS = 16
LAG = 2
PIECES = 2
MESH = pl.DeviceIdType.MESH
F32 = jnp.float32
BF16 = jnp.bfloat16


def groups_of(n, parts, b):
    if parts % 2 or parts < 6:
        return [(c, 1) for c in range(parts)]
    if b == n - 1:
        return [(0, 1), (1, 1)] + [(c, 2) for c in range(2, parts, 2)]
    return [(c, 2) for c in range(0, parts, 2)]


def unit_order(n, parts):
    blocks = [[(b, *g) for g in groups_of(n, parts, b)] for b in range(n)]
    units = [u for b in range(max(n - 2, 0)) for u in blocks[b]]
    late = len(units)
    units += blocks[n - 2][:1]
    last = len(units)
    units += blocks[n - 1][:1]
    for pair in zip(blocks[n - 2][1:], blocks[n - 1][1:]):
        units += pair
    return units, late, last


def mix_kernel(
    n, m, nd, ng, pieces,
    len_ref, q_hbm, k_hbm, v_hbm, route_hbm, numer_hbm, res_hbm, gain_hbm, w_ref, wg_ref, wu_ref,
    own_ref, out_ref,
    q_ref, route_ref, numer_ref, res_ref, gain_ref,
    st, metas, meta_ref, tiles, acc, rows, sq, picks, gates,
    kvbuf, wbuf, cut, abuf, pbuf, sbuf, up, cross, hid,
    in_s, kv_s, kv_r, me_s, me_r, w_s, w_r, wy_s, wy_r, wd_s, wd_r, wl,
    a_s, a_r, af_s, af_r, s_s, s_r, c_r, t_s, t_r, x_s, x_r, tile_s, out_s,
):
    z = lax.axis_index("seq")
    x = lax.axis_index("head")
    c_me = lax.axis_index("dat")
    g_me = lax.axis_index("grp")
    tok, share = res_ref.shape
    heads = q_ref.shape[1] // HEAD_SIZE
    kv = kvbuf.shape[2] // 2
    groups = kv // HEAD_SIZE
    per = heads // groups
    width = HEAD_SIZE // n
    parts, cw = st.shape[2], st.shape[4]
    depth = abuf.shape[3]
    cuts = 2 if parts % 2 == 0 else 1
    ww = share // cuts
    experts, hidden = acc.shape[0], acc.shape[3]
    ring = tiles.shape[0]
    half = n // 2
    batch = 4 if n % 4 == 0 else n
    span, part_slots = batch * tok, batch * MOST

    lower = z < half
    inner = jnp.where(lower, z + 1, z - 1)
    outer = jnp.where(lower, z - 1, z + 1)
    middle = (z == half - 1) | (z == half)
    has_outer = (z > 0) & (z < n - 1)

    def peer(me, k, size):
        return lax.rem(me + k, size)

    def source(me, k, size):
        return lax.rem(me - k + size, size)

    sends = []

    def remote(src, dst, s_sem, r_sem, where):
        return pltpu.make_async_remote_copy(
            src_ref=src, dst_ref=dst, send_sem=s_sem, recv_sem=r_sem,
            device_id=where, device_id_type=MESH,
        )

    def send(src, dst, s_sem, r_sem, where, cond=None):
        make = functools.partial(remote, src, dst, s_sem, r_sem, where)
        if cond is None:
            make().start()
        else:
            pl.when(cond)(lambda: make().start())
        sends.append((cond, make))

    def arrived(dst, r_sem, where):
        remote(dst, dst, in_s.at[0], r_sem, where).wait_recv()

    order = [(c, e, u) for c in range(parts) for e in range(experts) for u in range(2)]

    def tile_copies(q):
        c, e, u = order[q]
        return [
            pltpu.make_async_copy(
                (wg_ref, wu_ref)[u].at[e, pl.ds(h * share + c * cw, cw), :],
                tiles.at[q % ring, pl.ds(h * cw, cw), :],
                tile_s.at[q % ring, h],
            )
            for h in range(m)
        ]

    barrier = pltpu.get_barrier_semaphore()
    count = 0
    for axis, me, size in (("seq", z, n), ("head", x, m), ("dat", c_me, nd), ("grp", g_me, ng)):
        for k in range(1, size):
            pl.semaphore_signal(barrier, inc=1, device_id={axis: peer(me, k, size)}, device_id_type=MESH)
            count += 1
    loads = [
        pltpu.make_async_copy(src, dst, in_s.at[i])
        for i, (src, dst) in enumerate((
            (k_hbm, kvbuf.at[z, :, pl.ds(0, kv)]), (v_hbm, kvbuf.at[z, :, pl.ds(kv, kv)]), (q_hbm, q_ref),
            (route_hbm, route_ref), (numer_hbm, numer_ref), (res_hbm, res_ref), (gain_hbm, gain_ref),
        ))
    ]
    for load in loads:
        load.start()
    own_w = []
    for c in range(cuts):
        start = pl.multiple_of(x * share + c * ww, 128)
        own_w.append(pltpu.make_async_copy(
            w_ref.at[:, pl.ds(start, ww)], wbuf.at[x, :, pl.ds(c * ww, ww)], wl.at[c]
        ))
        own_w[-1].start()
    filled = min(ring, len(order))
    for q in range(filled // 3):
        for copy in tile_copies(q):
            copy.start(priority=1)
    for s in range(n):
        @pl.when(s > z)
        def _(s=s):
            kvbuf[s] = jnp.zeros(kvbuf.shape[1:], BF16)
    for load in loads:
        load.wait()
    meta_ref[0:2] = route_ref[...].astype(F32)
    meta_ref[2:3] = numer_ref[...].astype(F32)
    meta_ref[3:8] = jnp.zeros((5, tok), F32)
    metas[z] = meta_ref[...]
    pl.semaphore_wait(barrier, count)

    for k in range(n - 1, 0, -1):
        to = jnp.minimum(z + k, n - 1)
        send(kvbuf.at[z], kvbuf.at[z], kv_s.at[k - 1], kv_r.at[z], {"seq": to}, z + k < n)
    w_rows = depth // pieces
    piece = g_me * nd + c_me if pieces > 1 else 0

    def w_block(h, c, p):
        return wbuf.at[h, pl.ds(pl.multiple_of(p * w_rows, w_rows), w_rows), pl.ds(c * ww, ww)]

    for c in range(cuts):
        for j in range(1, m):
            to = peer(x, j, m)
            start = pl.multiple_of(to * share + c * ww, 128)
            src = w_ref.at[pl.ds(pl.multiple_of(piece * w_rows, w_rows), w_rows), pl.ds(start, ww)]
            send(src, w_block(x, c, piece), w_s.at[j - 1, c], w_r.at[j - 1, c], {"head": to})
    for k in range(1, n):
        send(meta_ref, metas.at[z], me_s.at[k - 1], me_r.at[z], {"seq": peer(z, k, n)})

    def w_over_x(c):
        for j in range(1, m):
            s = source(x, j, m)
            block = w_block(s, c, piece)
            arrived(block, w_r.at[j - 1, c], {"head": s})
            if pieces > 1:
                for k in range(1, ng):
                    send(block, block, wy_s.at[j - 1, c, k - 1], wy_r.at[j - 1, c, k - 1], {"grp": peer(g_me, k, ng)})
                for i in range(1, nd):
                    send(block, block, wd_s.at[j - 1, c, i - 1, 0], wd_r.at[j - 1, c, i - 1, 0], {"dat": peer(c_me, i, nd)})

    def w_over_y(c):
        if pieces == 1:
            return
        for j in range(1, m):
            s = source(x, j, m)
            for k in range(1, ng):
                g = source(g_me, k, ng)
                block = w_block(s, c, g * nd + c_me)
                arrived(block, wy_r.at[j - 1, c, k - 1], {"grp": g})
                for i in range(1, nd):
                    send(block, block, wd_s.at[j - 1, c, i - 1, k], wd_r.at[j - 1, c, i - 1, k], {"dat": peer(c_me, i, nd)})

    def w_ready(c):
        own_w[c].wait()
        if pieces == 1:
            return
        for j in range(1, m):
            s = source(x, j, m)
            for i in range(1, nd):
                d = source(c_me, i, nd)
                for k in range(ng):
                    g = source(g_me, k, ng)
                    arrived(w_block(s, c, g * nd + d), wd_r.at[j - 1, c, i - 1, k], {"dat": d})

    def attend():
        row = lax.broadcasted_iota(jnp.int32, (per * tok, n * tok), 0)
        col = lax.broadcasted_iota(jnp.int32, (per * tok, n * tok), 1)
        allowed = (col <= lax.rem(row, tok) + z * tok) & (col < len_ref[0])
        scale = 1.0 / math.sqrt(HEAD_SIZE)
        done = []
        for g in range(groups):
            lanes = slice(g * HEAD_SIZE, (g + 1) * HEAD_SIZE)
            queries = jnp.concatenate(
                [q_ref[:, (g * per + i) * HEAD_SIZE : (g * per + i + 1) * HEAD_SIZE] for i in range(per)], axis=0
            )
            keys = kvbuf[:, :, lanes].reshape(n * tok, HEAD_SIZE)
            vals = kvbuf[:, :, kv + g * HEAD_SIZE : kv + (g + 1) * HEAD_SIZE].reshape(n * tok, HEAD_SIZE)
            scores = lax.dot_general(queries, keys, (((1,), (1,)), ((), ())), preferred_element_type=F32) * scale
            scores = jnp.where(allowed, scores, NEG)
            top = jnp.max(scores, axis=1, keepdims=True)
            probs = jnp.where(allowed, jnp.exp(scores - top), 0.0)
            denom = jnp.sum(probs, axis=1, keepdims=True)
            mixed = jnp.dot(probs.astype(BF16), vals, preferred_element_type=F32)
            done.append((mixed / denom).astype(BF16))
        for d in range(n):
            cut[d] = jnp.concatenate(
                [
                    done[g][i * tok : (i + 1) * tok, d * width : (d + 1) * width]
                    for g in range(groups)
                    for i in range(per)
                ],
                axis=1,
            )
        abuf[x, z] = cut[z]

    def attention_sends():
        out = []
        for k in range(1, n):
            to = peer(z, k, n)
            out.append((cut.at[to], abuf.at[x, z], a_s.at[k - 1], a_r.at[z], {"seq": to}))
        for j in range(1, m):
            out.append((cut.at[z], abuf.at[x, z], af_s.at[j - 1, z], af_r.at[j - 1, z], {"head": peer(x, j, m)}))
        return out

    def attention_at(cond):
        @pl.when(cond)
        def _():
            for s in range(n):
                @pl.when(s < z)
                def _(s=s):
                    arrived(kvbuf.at[s], kv_r.at[s], {"seq": s})

            attend()
            for item in attention_sends():
                remote(*item).start()

    def forward(b):
        @pl.when(z != b)
        def _():
            arrived(abuf.at[x, b], a_r.at[b], {"seq": b})
            for j in range(1, m):
                remote(
                    abuf.at[x, b], abuf.at[x, b], af_s.at[j - 1, b], af_r.at[j - 1, b], {"head": peer(x, j, m)}
                ).start()

    def a_ready(b):
        for j in range(1, m):
            h = source(x, j, m)
            arrived(abuf.at[h, b], af_r.at[j - 1, b], {"head": h})

    def project(b, c, k):
        cols = slice(c * cw, (c + k) * cw)
        total = res_ref[:, cols].astype(F32) * (z == b).astype(F32)
        for h in range(m):
            total = total + jnp.dot(abuf[h, b], wbuf[h, :, cols], preferred_element_type=F32)
        for i in range(k):
            pbuf[b, c + i] = total[:, i * cw : (i + 1) * cw]

    def to_inner(b, c, k):
        def start(dst, r_sem):
            remote(sbuf.at[b, pl.ds(c, k)], dst.at[b, pl.ds(c, k)], s_s.at[b, c], r_sem.at[b, c], {"seq": inner}).start()

        pl.when(middle)(lambda: start(cross, c_r))
        if n > 2:
            pl.when(jnp.logical_not(middle))(lambda: start(up, s_r))

    def first(b, c, k):
        sbuf[b, c : c + k] = pbuf[b, c : c + k].astype(BF16)
        to_inner(b, c, k)

    def inwards(b, c, k):
        own = slice(c, c + k)
        arrived(up.at[b, pl.ds(c, k)], s_r.at[b, c], {"seq": outer})
        sbuf[b, own] = (pbuf[b, own] + up[b, own].astype(F32)).astype(BF16)
        to_inner(b, c, k)

    def outwards(b, c, k):
        mine = st.at[x, b, pl.ds(c, k)]
        own = slice(c, c + k)

        @pl.when(middle)
        def _():
            arrived(cross.at[b, pl.ds(c, k)], c_r.at[b, c], {"seq": inner})
            st[x, b, own] = (sbuf[b, own].astype(F32) + cross[b, own].astype(F32)).astype(BF16)

        if n > 2:
            @pl.when(jnp.logical_not(middle))
            def _():
                arrived(mine, t_r.at[b, c], {"seq": inner})

            @pl.when(has_outer)
            def _():
                remote(mine, mine, t_s.at[b, c], t_r.at[b, c], {"seq": outer}).start()
        for j in range(1, m):
            remote(mine, mine, x_s.at[j - 1, b, c], x_r.at[j - 1, b, c], {"head": peer(x, j, m)}).start()

    def routing():
        for s in range(n):
            @pl.when(s != z)
            def _(s=s):
                arrived(metas.at[s], me_r.at[s], {"seq": s})
        r_id = lax.broadcasted_iota(jnp.int32, (span, span), 0)
        c_id = lax.broadcasted_iota(jnp.int32, (span, span), 1)
        before = ((r_id < c_id) & (r_id // tok == c_id // tok)).astype(BF16)
        slot_id = lax.broadcasted_iota(jnp.int32, (part_slots, span), 0)
        base = (lax.broadcasted_iota(jnp.int32, (1, span), 1) // tok) * MOST
        for b in range(n // batch):
            meta = jnp.concatenate([metas[b * batch + i] for i in range(batch)], axis=1)
            weight = meta[2:3] / 256.0
            for e in range(experts):
                this = (x * experts + e).astype(F32)
                gate = jnp.where(meta[0:1] == this, weight, 0.0) + jnp.where(meta[1:2] == this, 1.0 - weight, 0.0)
                marked = gate > 0
                spread = jnp.broadcast_to(jnp.where(marked, 1.0, 0.0), (8, span)).astype(BF16)
                rank = jnp.dot(spread, before, preferred_element_type=F32)[0:1].astype(jnp.int32)
                pick = jnp.where(slot_id == jnp.where(marked, rank + base, -1), 1.0, 0.0)
                picks[b, e * part_slots : (e + 1) * part_slots] = pick.astype(BF16)
                gates[e, b * part_slots : (b + 1) * part_slots] = jnp.sum(pick * gate, axis=1, keepdims=True)

    def gather(c):
        for b, first_c, k in units:
            if first_c == c:
                for j in range(1, m):
                    h = source(x, j, m)
                    arrived(st.at[h, b, pl.ds(c, k)], x_r.at[j - 1, b, c], {"head": h})
        for h in range(m):
            start = h * share + c * cw
            gain = gain_ref[start : start + cw].astype(F32).reshape(1, cw)
            for b in range(n // batch):
                block = st[h, b * batch : (b + 1) * batch, c].reshape(span, cw)
                raw = jnp.dot(picks[b], block, preferred_element_type=F32)
                square = raw * raw
                folded = square[:, 0:128]
                for i in range(1, cw // 128):
                    folded = folded + square[:, i * 128 : (i + 1) * 128]
                scaled = (raw * gain).astype(BF16)
                own = slice(b * part_slots, (b + 1) * part_slots)
                for e in range(experts):
                    mine = slice(e * part_slots, (e + 1) * part_slots)
                    rows[e, own, h * cw : (h + 1) * cw] = scaled[mine]
                    if c == 0 and h == 0:
                        sq[e, own] = folded[mine]
                    else:
                        sq[e, own] += folded[mine]

    def in_batches(f):
        if n == batch:
            f(slice(None))
        else:
            pl.loop(0, n // batch)(lambda b: f(pl.ds(pl.multiple_of(b * part_slots, part_slots), part_slots)))

    def tile_of(c, e, u):
        return (c * experts + e) * 2 + u

    def multiply(c, e, u):
        q = tile_of(c, e, u)
        for copy in tile_copies(q):
            copy.wait()
        @in_batches
        def _(own):
            term = jnp.dot(rows[e, own], tiles[q % ring], preferred_element_type=F32)
            acc[e, u, own] = term if c == 0 else acc[e, u, own] + term
        if q + ring < len(order):
            for copy in tile_copies(q + ring):
                copy.start(priority=1)

    def finish(c, e):
        for u in range(2):
            for copy in tile_copies(tile_of(c, e, u)):
                copy.wait()
        step = min(hidden, 512)

        @in_batches
        def _(own):
            factor = lax.rsqrt(jnp.sum(sq[e, own], axis=1, keepdims=True) / (m * share) + EPS)
            for t in range(hidden // step):
                cols = slice(t * step, (t + 1) * step)
                part = []
                for u in range(2):
                    term = jnp.dot(rows[e, own], tiles[tile_of(c, e, u) % ring, :, cols], preferred_element_type=F32)
                    part.append((term if c == 0 else acc[e, u, own, cols] + term) * factor)
                act = part[0] / (1.0 + jnp.exp(-part[0]))
                hid[e, own, cols] = (gates[e, own] * (act * part[1])).astype(BF16)

        copy = pltpu.make_async_copy(hid.at[e], out_ref.at[e, 0], out_s.at[e])
        copy.start()
        return copy

    units, late, last = unit_order(n, parts)
    at_end = jnp.logical_not(has_outer)

    def of_block(b):
        return [u for u in units if u[0] == b]

    def run(cond, events):
        if events:
            @pl.when(cond)
            def _():
                for f, u in events:
                    f(*u)

    def start_sum(b, c):
        if b < n - 1:
            run(at_end, [(first, u) for u in units[:last] if u[0] == b and u[1] + u[2] - 1 == c])
        elif c == parts - 1:
            run(at_end, [(first, u) for u in units[last:]])

    def stage(b):
        a_ready(b)
        project(b, 0, parts)
        for c in range(parts):
            start_sum(b, c)

    attention_at(z == 0)
    over_x = [functools.partial(w_over_x, c) for c in range(cuts)]
    over_x.pop(0)()
    forward(0)
    attention_at(z == 1)
    for f in over_x[:1]:
        f()
    if n > 2:
        attention_at(z >= 2)
    for f in over_x[1:]:
        f()
    later = [functools.partial(forward, b) for b in range(1, n)]
    for c in range(cuts):
        w_over_y(c)
        w_ready(c)
        if c == 0:
            a_ready(0)
        project(0, c * (parts // cuts), parts // cuts)
        for i in range(c * (parts // cuts), (c + 1) * (parts // cuts)):
            start_sum(0, i)
        if len(later) > 1:
            later.pop(0)()
    for f in later:
        f()
    for q in range(filled // 3, filled):
        for copy in tile_copies(q):
            copy.start(priority=1)
    for b in range(1, n):
        events = []
        for i in range(parts):
            if b >= 3:
                events += [(outwards, u) for u in of_block(b - 3)[i : i + 1]]
            if b >= 2:
                events += [(inwards, u) for u in of_block(b - 2)[i : i + 1]]
        run(has_outer, events)
        stage(b)
    routing()

    run(at_end, [(outwards, u) for u in units[:late]])
    todo = units[late:]
    if n >= 3:
        events = []
        for u in of_block(n - 3):
            events += [(outwards, u)] + [(inwards, v) for v in todo[:1]]
            todo = todo[1:]
        run(has_outer, events)
    else:
        todo = []
    ready = [max(i for i, u in enumerate(units) if u[1] <= c < u[1] + u[2]) for c in range(parts)]
    work = []
    for c in range(parts - 1):
        work.append((ready[c] + LAG, functools.partial(gather, c)))
        for e in range(experts):
            work.append((ready[c] + LAG, functools.partial(multiply, c, e, 0)))
            work.append((ready[c] + LAG, functools.partial(multiply, c, e, 1)))
    for j in range(late, len(units)):
        run(has_outer, [(inwards, v) for v in todo[:1]])
        todo = todo[1:]
        outwards(*units[j])
        for _ in range(PIECES):
            if work and work[0][0] <= j:
                work.pop(0)[1]()
    for _, f in work:
        f()
    gather(parts - 1)
    outs = []
    for c in range(parts):
        outs.append(pltpu.make_async_copy(st.at[x, z, c], own_ref.at[:, pl.ds(c * cw, cw)], out_s.at[experts + c]))
        outs[-1].start()
    for e in range(experts):
        outs.append(finish(parts - 1, e))

    for cond, make in sends:
        if cond is None:
            make().wait_send()
        else:
            pl.when(cond)(lambda make=make: make().wait_send())

    for item in attention_sends():
        remote(*item).wait_send()
    for b in range(n):
        @pl.when(z != b)
        def _(b=b):
            for j in range(1, m):
                remote(
                    abuf.at[x, b], abuf.at[x, b], af_s.at[j - 1, b], af_r.at[j - 1, b], {"head": peer(x, j, m)}
                ).wait_send()
    for b, c, k in units:
        own = sbuf.at[b, pl.ds(c, k)]
        remote(own, own, s_s.at[b, c], s_r.at[b, c], {"seq": inner}).wait_send()
        mine = st.at[x, b, pl.ds(c, k)]
        if n > 2:
            @pl.when(has_outer)
            def _(b=b, c=c, mine=mine):
                remote(mine, mine, t_s.at[b, c], t_r.at[b, c], {"seq": outer}).wait_send()
        for j in range(1, m):
            remote(mine, mine, x_s.at[j - 1, b, c], x_r.at[j - 1, b, c], {"head": peer(x, j, m)}).wait_send()
    for copy in outs:
        copy.wait()


def place_kernel(own_ref, hidden_ref, own_out, hidden_out, own_buf, hidden_buf, sems):
    experts = hidden_ref.shape[0]
    moves = [(own_ref, own_buf, own_out)]
    moves += [(hidden_ref.at[e], hidden_buf.at[e], hidden_out.at[e]) for e in range(experts)]
    loads = [pltpu.make_async_copy(src, buf, sems.at[0, i]) for i, (src, buf, _) in enumerate(moves)]
    stores = [pltpu.make_async_copy(buf, dst, sems.at[1, i]) for i, (_, buf, dst) in enumerate(moves)]
    for load in loads:
        load.start()
    for load, store in zip(loads, stores):
        load.wait()
        store.start()
    for store in stores:
        store.wait()


def local(
    n, m, nd, ng,
    queries, keys, values, residual_in, out_proj, norm_gain,
    expert_gate, expert_up, routes, gate_numer, sequence_lengths,
):
    tok, feats = queries.shape[1:]
    kv = keys.shape[2]
    share = residual_in.shape[2]
    heads, width, features = out_proj.shape
    depth = heads * width
    experts, _, hidden = expert_gate.shape
    slots = n * MOST
    batch = 4 if n % 4 == 0 else n
    parts = max(p for p in range(1, share // 128 + 1) if share % (128 * p) == 0 and (p == 1 or n * p <= UNITS))
    cw = share // parts
    pieces = ng * nd if depth % (16 * ng * nd) == 0 else 1
    ring = min(2 * parts * experts, RING_BYTES // (2 * m * cw * hidden))
    vmem = pl.BlockSpec(memory_space=pltpu.VMEM)
    hbm = pl.BlockSpec(memory_space=pl.ANY)
    dma = pltpu.SemaphoreType.DMA
    own, hidden_out = pl.pallas_call(
        functools.partial(mix_kernel, n, m, nd, ng, pieces),
        out_shape=(
            jax.ShapeDtypeStruct((tok, share), BF16),
            jax.ShapeDtypeStruct((experts, 1, slots, hidden), BF16),
        ),
        in_specs=[pl.BlockSpec(memory_space=pltpu.SMEM)] + [hbm] * 10,
        out_specs=(hbm, hbm),
        scratch_shapes=[
            pltpu.VMEM((tok, feats), BF16),
            pltpu.VMEM((2, tok), jnp.int32),
            pltpu.VMEM((1, tok), jnp.int32),
            pltpu.VMEM((tok, share), BF16),
            pltpu.VMEM((features,), BF16),
            pltpu.VMEM((m, n, parts, tok, cw), BF16),
            pltpu.VMEM((n, 8, tok), F32),
            pltpu.VMEM((8, tok), F32),
            pltpu.VMEM((ring, m * cw, hidden), BF16),
            pltpu.VMEM((experts, 2, slots, hidden), F32),
            pltpu.VMEM((experts, slots, m * cw), BF16),
            pltpu.VMEM((experts, slots, 128), F32),
            pltpu.VMEM((n // batch, experts * batch * MOST, batch * tok), BF16),
            pltpu.VMEM((experts, slots, 1), F32),
            pltpu.VMEM((n, tok, 2 * kv), BF16),
            pltpu.VMEM((m, depth, share), BF16),
            pltpu.VMEM((n, tok, depth), BF16),
            pltpu.VMEM((m, n, tok, depth), BF16),
            pltpu.VMEM((n, parts, tok, cw), F32),
            pltpu.VMEM((n, parts, tok, cw), BF16),
            pltpu.VMEM((n, parts, tok, cw), BF16),
            pltpu.VMEM((n, parts, tok, cw), BF16),
            pltpu.VMEM((experts, slots, hidden), BF16),
            dma((7,)),
            dma((n - 1,)), dma((n,)),
            dma((n - 1,)), dma((n,)),
            dma((m - 1, parts)), dma((m - 1, parts)),
            dma((m - 1, parts, max(ng - 1, 1))), dma((m - 1, parts, max(ng - 1, 1))),
            dma((m - 1, parts, max(nd - 1, 1), ng)), dma((m - 1, parts, max(nd - 1, 1), ng)),
            dma((parts,)),
            dma((n - 1,)), dma((n,)), dma((m - 1, n)), dma((m - 1, n)),
            dma((n, parts)), dma((n, parts)), dma((n, parts)),
            dma((n, parts)), dma((n, parts)),
            dma((m - 1, n, parts)), dma((m - 1, n, parts)),
            dma((ring, m)), dma((experts + parts,)),
        ],
        compiler_params=pltpu.CompilerParams(
            collective_id=0, has_side_effects=True, vmem_limit_bytes=63 * 1024 * 1024
        ),
    )(
        sequence_lengths, queries[0], keys[0], values[0], routes[0].T, gate_numer, residual_in[0],
        norm_gain, out_proj.reshape(depth, features), expert_gate, expert_up,
    )
    own, hidden_out = pl.pallas_call(
        place_kernel,
        out_shape=tuple(jax.ShapeDtypeStruct(a.shape, a.dtype) for a in (own, hidden_out)),
        in_specs=[hbm, hbm],
        out_specs=(hbm, hbm),
        scratch_shapes=[
            pltpu.VMEM(own.shape, BF16), pltpu.VMEM(hidden_out.shape, BF16), dma((2, 1 + experts)),
        ],
    )(own, hidden_out)
    return (own[None], hidden_out)


def solution(mesh):
    seq_spec = P(("grp", "dat"), "seq", "head")
    in_specs = (
        seq_spec, seq_spec, seq_spec, seq_spec,
        P("head", "seq", None), P(),
        P("head", None, "seq"), P("head", None, "seq"),
        P(("grp", "dat"), "seq", None), P(("grp", "dat"), "seq"), P(("grp", "dat")),
    )
    out_specs = (seq_spec, P("head", ("grp", "dat"), None, "seq"))
    sizes = [mesh.shape[axis] for axis in ("seq", "head", "dat", "grp")]
    body = functools.partial(local, *sizes)
    return jax.shard_map(body, mesh=mesh, in_specs=in_specs, out_specs=out_specs, check_vma=False)
```
